128 devices in a mesh: cells: 64 (over z, x_hi, y, core), waves: 2 (over x_lo).
Axes of the slice: x: 4 (x_hi: 2, x_lo: 2; x = x_hi * 2 + x_lo), y: 4, z: 4, core: 2. Of those that a mesh axis runs over, the one named last changes fastest.
Arguments:
- features: bfloat16 [131072, 512], P('cells', 'waves'), may hold values from -6 to 6
- positions: float32 [3, 131072], P(None, 'cells'), may hold values from 0 to 1024, as said below
- occupancy: int32 [1024], P('cells'), may hold values from 1 to 128, as said below
- neighbours: int32 [1024, 3], P('cells'), may hold values from -2 to 2, as said below
- wavevectors: float32 [3, 4096], P(None, 'waves'), may hold values from -1 to 1
- filters: float32 [4096, 512], P('waves'), may hold values from -6 to 6
- falloffs: float32 [4], replicated, may hold values from 0.05 to 2
- mixing: float32 [4, 512], replicated, may hold values from -2 to 2
- norm_gain: float32 [512], replicated, may hold values from 0.5 to 1.5
- in_weight: bfloat16 [512, 1024], P(None, 'waves'), may hold values from -0.25 to 0.25
- out_weight: bfloat16 [1024, 512], P('waves'), may hold values from -0.1875 to 0.1875
Outputs:
- result: bfloat16 [131072, 512], P('cells', 'waves')
The draws below stay inside these ranges and needn't reach their ends.
Inputs may be any that keep to these rules, and one draw needn't show every extreme that they name: `occupancy`: the atoms of a cell fill its first slots; the last cell is full. `neighbours`: each row holds 3 distinct offsets; cell c interacts with cells c + offset modulo 1024. `positions`: the first coordinate of an atom in cell c lies in [c, c + 1]; the other two lie in [0, 3].
All inputs are finite; a program needn't handle non-finite values.
Results may differ from the reference program's by a relative error of at most 0.009.
Values may be sent and summed in bfloat16 or wider, within the bound.
A program may use at most 128 MiB of HBM per device.

```python
import math
import jax
import jax.numpy as jnp
from jax import lax

F = 512
H = 1024
K = 4096
G = 4
CAP = 128
NB = 3
HW = 2
NCELLS = 1024
ATOMS = 131072


def draw_positions(key, part):
    key_along, key_across = jax.random.split(key)
    along = jax.random.uniform(key_along, (ATOMS,), jnp.float32)
    cell_number = (jnp.arange(ATOMS, dtype=jnp.int32) // CAP).astype(jnp.float32)
    across = jax.random.uniform(key_across, (2, ATOMS), jnp.float32) * 3.0
    return jnp.concatenate([(cell_number + along)[None, :], across], axis=0)


def draw_occupancy(key, part):
    key_fill, key_counts = jax.random.split(key)
    fill_level = jax.random.randint(key_fill, (), 102, 257)
    cell_number = jnp.arange(NCELLS, dtype=jnp.int32)
    ramp = CAP // 3 + (CAP - CAP // 3) * cell_number // max(NCELLS - 1, 1)
    ceiling = jnp.maximum(ramp * fill_level // 256, 1)
    floor_count = jnp.maximum(3 * ceiling // 4, 1)
    drawn = jax.random.randint(key_counts, (NCELLS,), floor_count, ceiling + 1)
    return drawn.at[NCELLS - 1].set(CAP).astype(jnp.int32)


def draw_neighbours(key, part):
    span_count = 2 * HW + 1
    scores = jax.random.randint(key, (NCELLS, span_count), 0, 4096) * span_count + jnp.arange(span_count, dtype=jnp.int32)[None, :]
    ranked = jnp.argsort(scores, axis=1)
    return (ranked[:, :NB] - HW).astype(jnp.int32)


def level_of(own_key, extent, shards, low, high):
    loudness, own = 1.0, jax.random.fold_in(own_key, 6)
    for position, blocks in shards:
        steps = jnp.exp(jax.random.uniform(jax.random.fold_in(own, position), (blocks,), jnp.float32, low / len(shards), high / len(shards)))
        loudness = loudness * jnp.repeat(steps, extent[position] // blocks).reshape([-1 if axis == position else 1 for axis in range(len(extent))])
    return loudness


def normal_values(key, extent, width, reach, cuts=(), held_as=jnp.bfloat16):
    array = jax.random.normal(key, extent, jnp.float32) * width
    if len(cuts) > 0:
        array = level_of(key, extent, cuts, -0.22, 0.18) * array
    return jnp.clip(array, min=-reach, max=reach).astype(held_as)


def setup_inputs(seed: int = 0) -> dict:
    arg_keys = jax.random.split(jax.random.key(seed), 12)
    features = normal_values(arg_keys[0], (ATOMS, F), 1.0, 6.0, ((0, 64), (1, 2)))
    positions = draw_positions(jax.random.fold_in(arg_keys[11], 71), 0)
    occupancy = draw_occupancy(jax.random.fold_in(arg_keys[11], 71), 0)
    neighbours = draw_neighbours(jax.random.fold_in(arg_keys[11], 71), 0)
    wavevectors = jnp.clip(jax.random.uniform(arg_keys[4], (3, K), jnp.float32, -1.0, 1.0) * level_of(arg_keys[4], (3, K), ((1, 2),), -0.4, 0.0), -1.0, 1.0)
    filters = normal_values(arg_keys[5], (K, F), 1.0, 6.0, ((0, 2),), jnp.float32)
    falloffs = jnp.clip(jnp.exp(jax.random.uniform(arg_keys[6], (G,), jnp.float32, math.log(0.05), math.log(2.0))), 0.05, 2.0)
    mixing = normal_values(arg_keys[7], (G, F), 0.15, 2.0, (), jnp.float32)
    norm_gain = jnp.clip(1.0 + 0.1 * jax.random.normal(arg_keys[8], (F,), jnp.float32), 0.5, 1.5)
    in_weight = normal_values(arg_keys[9], (F, H), F ** -0.5, 0.25, ((1, 2),))
    out_weight = normal_values(arg_keys[10], (H, F), H ** -0.5, 0.1875, ((0, 2),))
    return {"features": features, "positions": positions, "occupancy": occupancy, "neighbours": neighbours, "wavevectors": wavevectors, "filters": filters, "falloffs": falloffs, "mixing": mixing, "norm_gain": norm_gain, "in_weight": in_weight, "out_weight": out_weight}


EPS = 1e-06

def wrap_long(along_x, length):
    return jnp.where(along_x > 0.5 * length, along_x - length, jnp.where(along_x < -0.5 * length, along_x + length, along_x))

def phases_of(block_waves, positions):
    return block_waves[0][:, None] * positions[0][None, :] + block_waves[1][:, None] * positions[1][None, :] + block_waves[2][:, None] * positions[2][None, :]

def near_part(masked, positions, neighbours, falloffs, mixing):
    cell_feats = masked.reshape(NCELLS, CAP, F)
    cell_pos = positions.reshape(3, NCELLS, CAP)
    length = jnp.float32(NCELLS)

    def one_cell(cell_index):
        local_pos = cell_pos[:, cell_index]
        summed = jnp.zeros((G, CAP, F), jnp.float32)
        for neighbour in range(NB):
            partner = (cell_index + neighbours[cell_index, neighbour]) % NCELLS
            other_pos = cell_pos[:, partner]
            displace = local_pos[:, :, None] - other_pos[:, None, :]
            along_x = wrap_long(displace[0], length)
            squared = along_x * along_x + displace[1] * displace[1] + displace[2] * displace[2]
            kernel = jnp.exp(-falloffs[:, None, None] * squared[None]).astype(jnp.bfloat16)
            summed = summed + jnp.einsum('gij,jf->gif', kernel.astype(jnp.float32), cell_feats[partner].astype(jnp.float32), precision=lax.Precision.HIGHEST)
        return lax.optimization_barrier(jnp.sum(summed * mixing[:, None, :], axis=0))
    return lax.map(one_cell, jnp.arange(NCELLS, dtype=jnp.int32)).reshape(NCELLS * CAP, F)

def trig_wide(block_waves, positions):
    phases = phases_of(block_waves, positions)
    cosine_block = lax.optimization_barrier(jnp.cos(phases).astype(jnp.bfloat16)).astype(jnp.float32)
    sine_block = lax.optimization_barrier(jnp.sin(phases).astype(jnp.bfloat16)).astype(jnp.float32)
    return (cosine_block, sine_block)

def far_part(masked, positions, wavevectors, filters, count):
    block_rows = math.gcd(K, 512)
    stacked = wavevectors.reshape(3, K // block_rows, block_rows).transpose(1, 0, 2)
    masked_wide = masked.astype(jnp.float32)

    def forward(block_waves):
        cosine_block, sine_block = trig_wide(block_waves, positions)
        return (jnp.dot(cosine_block, masked_wide, precision=lax.Precision.HIGHEST), jnp.dot(sine_block, masked_wide, precision=lax.Precision.HIGHEST))
    cos_factor, sin_factor = lax.map(forward, stacked)
    count_root = jnp.sqrt(count)
    cos_factor = cos_factor.reshape(K, F) / count_root
    sin_factor = sin_factor.reshape(K, F) / count_root
    cos_filtered = (filters * cos_factor).astype(jnp.bfloat16).reshape(K // block_rows, block_rows, F)
    sin_filtered = (filters * sin_factor).astype(jnp.bfloat16).reshape(K // block_rows, block_rows, F)

    def backward(running, pieces):
        block_waves, cos_rows, sin_rows = pieces
        cosine_block, sine_block = trig_wide(block_waves, positions)
        running = running + jnp.dot(cosine_block.T, cos_rows.astype(jnp.float32), precision=lax.Precision.HIGHEST)
        running = running + jnp.dot(sine_block.T, sin_rows.astype(jnp.float32), precision=lax.Precision.HIGHEST)
        return (running, None)
    far_sum, unused = lax.scan(backward, jnp.zeros((NCELLS * CAP, F), jnp.float32), (stacked, cos_filtered, sin_filtered))
    return far_sum / math.sqrt(K)

def reference(features, positions, occupancy, neighbours, wavevectors, filters, falloffs, mixing, norm_gain, in_weight, out_weight):
    slot_place = jnp.arange(NCELLS * CAP, dtype=jnp.int32) % CAP
    is_live = slot_place < jnp.repeat(occupancy, CAP)
    masked = jnp.where(is_live[:, None], features, jnp.zeros_like(features))
    count = jnp.sum(occupancy).astype(jnp.float32)
    near = near_part(masked, positions, neighbours, falloffs, mixing)
    far = far_part(masked, positions, wavevectors, filters, count)
    merged = features.astype(jnp.float32) + near + far
    normed = (merged * lax.rsqrt(lax.optimization_barrier(jnp.mean(merged * merged, axis=-1, keepdims=True)) + EPS) * norm_gain).astype(jnp.bfloat16)
    hidden = jax.nn.silu(jnp.dot(normed, in_weight, preferred_element_type=jnp.float32)).astype(jnp.bfloat16)
    result = merged + jnp.dot(hidden, out_weight, preferred_element_type=jnp.float32)
    return result.astype(jnp.bfloat16)
```

```python
import functools
import math

import jax
import jax.numpy as jnp
from jax import lax
from jax.experimental import pallas as pl
from jax.experimental.pallas import tpu as pltpu
from jax.sharding import PartitionSpec as P

F = 512
K = 4096
CAP = 128
HW = 2
NB = 3
G = 4
EPS = 1e-06
WAVES = 2
PART = 256
ROWS = 2048
LOCAL = 16
LENGTH = 1024.0
KP = 128
TILE = 256
CHUNK = 128
HALF = ROWS // 2
BF = jnp.bfloat16
F32 = jnp.float32
MESH = pl.DeviceIdType.MESH
TURN = 1.0 / (2.0 * math.pi)
LOG2E = 1.4426950408889634

SIN = (4.442867900911655, -7.307443330487869, 3.594787161239145, -0.784371485095076)
COS = (1.4142040799995839, -6.977641979004694, 5.715237169770743, -1.7283443233022544)


def params(**more):
    return pltpu.CompilerParams(vmem_limit_bytes=62 << 20, **more)


def split3(v):
    a = v.astype(BF).astype(F32)
    b = (v - a).astype(BF).astype(F32)
    c = ((v - a) - b).astype(BF).astype(F32)
    return a, b, c


def prologue(pos_ref, wave_ref, left_ref, right_ref, lrows, rrows):
    first = lax.axis_index("cells") * LOCAL
    lrows[...] = jnp.zeros_like(lrows)
    rrows[...] = jnp.zeros_like(rrows)
    cell = lax.broadcasted_iota(jnp.int32, (1, ROWS), 1) // CAP
    for part in range(3):
        v = pos_ref[part : part + 1, :]
        if part == 0:
            v = v - (cell + first).astype(F32)
        a, b, _ = split3(v)
        k1, k2, _ = split3(wave_ref[part : part + 1, :] * TURN)
        for n, (l, r) in enumerate(((a, k1), (a, k2), (b, k1), (b, k2))):
            row = part * 4 + n
            lrows[row : row + 1, :] = l
            rrows[row : row + 1, :] = r
    along = wave_ref[0:1, :] * TURN
    for c in range(LOCAL):
        whole = along * (first + c).astype(F32)
        whole = whole - lax.round(whole, lax.RoundingMethod.TO_NEAREST_EVEN)
        for n, piece in enumerate(split3(whole)):
            row = 12 + 3 * c + n
            lrows[row : row + 1, :] = (cell == c).astype(F32)
            rrows[row : row + 1, :] = piece
    left_ref[...] = lrows[...].T.astype(BF)
    right_ref[...] = rrows[...].astype(BF)


def phase_operands(positions, waves):
    return pl.pallas_call(
        prologue,
        out_shape=(
            jax.ShapeDtypeStruct((ROWS, KP), BF),
            jax.ShapeDtypeStruct((KP, K), BF),
        ),
        scratch_shapes=[pltpu.VMEM((KP, ROWS), F32), pltpu.VMEM((KP, K), F32)],
        compiler_params=params(),
    )(positions, waves)


def trig(turns):
    r = turns - lax.round(turns, lax.RoundingMethod.TO_NEAREST_EVEN)
    s = r * r
    half_sin = r * (SIN[0] + s * (SIN[1] + s * (SIN[2] + s * SIN[3])))
    half_cos = COS[0] + s * (COS[1] + s * (COS[2] + s * COS[3]))
    return (1.0 - half_sin * half_sin).astype(BF), (half_sin * half_cos).astype(BF)


def forward_kernel(left_ref, right_ref, feats_ref, cos_ref, sin_ref, sum_ref):
    cos_sum = jnp.zeros((PART, TILE), F32)
    sin_sum = jnp.zeros((PART, TILE), F32)
    for b in range(ROWS // TILE):
        rows = slice(b * TILE, (b + 1) * TILE)
        turns = jnp.dot(left_ref[rows, :], right_ref[...], preferred_element_type=F32)
        cosine, sine = trig(turns)
        cos_ref[rows, :] = cosine
        sin_ref[rows, :] = sine
        block = feats_ref[:, rows]
        cos_sum += jnp.dot(block, cosine, preferred_element_type=F32)
        sin_sum += jnp.dot(block, sine, preferred_element_type=F32)
    for n in range(TILE // CHUNK):
        lanes = slice(n * CHUNK, (n + 1) * CHUNK)
        sum_ref[0, n] = cos_sum[:, lanes].astype(BF)
        sum_ref[1, n] = sin_sum[:, lanes].astype(BF)


def forward(left, right, feats):
    return pl.pallas_call(
        forward_kernel,
        grid=(K // TILE,),
        in_specs=[
            pl.BlockSpec((ROWS, KP), lambda j: (0, 0)),
            pl.BlockSpec((KP, TILE), lambda j: (0, j)),
            pl.BlockSpec((PART, ROWS), lambda j: (0, 0)),
        ],
        out_specs=[
            pl.BlockSpec((ROWS, TILE), lambda j: (0, j)),
            pl.BlockSpec((ROWS, TILE), lambda j: (0, j)),
            pl.BlockSpec((2, TILE // CHUNK, PART, CHUNK), lambda j: (0, j, 0, 0)),
        ],
        out_shape=(
            jax.ShapeDtypeStruct((ROWS, K), BF),
            jax.ShapeDtypeStruct((ROWS, K), BF),
            jax.ShapeDtypeStruct((2, K // CHUNK, PART, CHUNK), BF),
        ),
        compiler_params=params(),
    )(left, right, feats)


def place():
    cells = lax.axis_index("cells")
    return cells // 16, (cells // 8) % 2, (cells // 2) % 4, cells % 2


def cell_index(z, x, y, core):
    return ((z * 2 + x) * 4 + y) * 2 + core


def exchange_kernel(
    sum_ref, filt_ref, feats_ref, pos_ref, count_ref, in_ref, out_ref,
    all_ref, in2_ref, out2_ref, edge_ref, edgepos_ref,
    r1, s1, r2a, r2b, s2a, s2b, r3a, r3b, s3a, s3b, r4a, r4b,
    mine, theirs, counts, rcounts, send_sem, recv_sem, local_sem,
):
    z, x, y, core = place()
    waves = lax.axis_index("waves")
    cells = lax.axis_index("cells")
    other = 1 - waves

    def at(cell):
        return {"cells": cell, "waves": waves}

    def sibling():
        return at(cell_index(z, x, y, 1 - core))

    def along_y(d):
        return at(cell_index(z, x, lax.rem(y + d, 4), core))

    def along_z(d):
        return at(cell_index(lax.rem(z + d, 4), x, y, core))

    def along_x():
        return at(cell_index(z, 1 - x, y, core))

    above = at(lax.rem(cells + 1, 64))
    below = at(lax.rem(cells + 63, 64))
    partner = {"cells": cells, "waves": other}
    peers = [sibling(), along_x(), partner, above, below]
    peers += [along_y(d) for d in (1, 2, 3)] + [along_z(d) for d in (1, 2, 3)]
    barrier = pltpu.get_barrier_semaphore()
    for peer in peers:
        pl.semaphore_signal(barrier, inc=1, device_id=peer, device_id_type=MESH)
    pl.semaphore_wait(barrier, len(peers))

    taken = [0]

    def remote(src, dst, device):
        n = taken[0]
        taken[0] += 1
        copy = pltpu.make_async_remote_copy(
            src_ref=src, dst_ref=dst, send_sem=send_sem.at[n], recv_sem=recv_sem.at[n],
            device_id=device, device_id_type=MESH,
        )
        copy.start()
        return copy

    one = [
        remote(sum_ref.at[1 - core], r1, sibling()),
        remote(count_ref, rcounts.at[0], sibling()),
    ]
    block = y * 8 + z * 2 + x
    row = pl.multiple_of(lax.rem(block, 16) * CHUNK, CHUNK)
    column = pl.multiple_of(other * PART, PART)
    own_column = pl.multiple_of(waves * PART, PART)
    early = [
        remote(filt_ref.at[pl.ds(row, CHUNK), pl.ds(column, PART)], theirs, partner),
        remote(feats_ref.at[pl.ds(0, 2 * CAP)], edge_ref.at[1], below),
        remote(feats_ref.at[pl.ds(ROWS - 2 * CAP, 2 * CAP)], edge_ref.at[0], above),
        remote(pos_ref.at[:, pl.ds(0, 2 * CAP)], edgepos_ref.at[1], below),
        remote(pos_ref.at[:, pl.ds(ROWS - 2 * CAP, 2 * CAP)], edgepos_ref.at[0], above),
        remote(in_ref, in2_ref, partner),
        remote(out_ref, out2_ref, partner),
    ]
    local = pltpu.make_async_copy(
        filt_ref.at[pl.ds(row, CHUNK), pl.ds(own_column, PART)], mine, local_sem
    )
    local.start()

    for copy in one:
        copy.wait()

    def add1(n, carry):
        yy, zz, xx = n // 8, (n // 2) % 4, n % 2
        s1[yy, zz, xx] = (
            sum_ref[core, yy, zz, xx].astype(F32) + r1[yy, zz, xx].astype(F32)
        ).astype(BF)
        return carry

    lax.fori_loop(0, 32, add1, 0)
    counts[0] = count_ref[...] + rcounts[0]

    two = []
    for d in (1, 2, 3):
        ty, tz = lax.rem(y + d, 4), lax.rem(z + d, 4)
        two += [
            remote(s1.at[ty, :, :, pl.ds(0, CHUNK), :], r2a.at[d - 1], along_y(d)),
            remote(s1.at[:, tz, :, pl.ds(CHUNK, CHUNK), :], r2b.at[d - 1], along_z(d)),
            remote(counts.at[0], rcounts.at[d], along_y(d)),
        ]
    for copy in two:
        copy.wait()

    def add2(n, carry):
        p, xx = n // 2, n % 2
        a = s1[y, p, xx, 0:CHUNK, :].astype(F32)
        b = s1[p, z, xx, CHUNK:PART, :].astype(F32)
        for d in range(3):
            a += r2a[d, p, xx].astype(F32)
            b += r2b[d, p, xx].astype(F32)
        s2a[p, xx] = a.astype(BF)
        s2b[p, xx] = b.astype(BF)
        return carry

    lax.fori_loop(0, 8, add2, 0)
    counts[1] = counts[0] + rcounts[1] + rcounts[2] + rcounts[3]

    three = []
    for d in (1, 2, 3):
        ty, tz = lax.rem(y + d, 4), lax.rem(z + d, 4)
        three += [
            remote(s2a.at[tz], r3a.at[d - 1], along_z(d)),
            remote(s2b.at[ty], r3b.at[d - 1], along_y(d)),
            remote(counts.at[1], rcounts.at[3 + d], along_z(d)),
        ]
    for copy in three:
        copy.wait()
    for xx in range(2):
        a, b = s2a[z, xx].astype(F32), s2b[y, xx].astype(F32)
        for d in range(3):
            a += r3a[d, xx].astype(F32)
            b += r3b[d, xx].astype(F32)
        s3a[xx] = a.astype(BF)
        s3b[xx] = b.astype(BF)
    counts[2] = counts[1] + rcounts[4] + rcounts[5] + rcounts[6]

    four = [
        remote(s3a.at[1 - x], r4a, along_x()),
        remote(s3b.at[1 - x], r4b, along_x()),
        remote(counts.at[2], rcounts.at[7], along_x()),
    ]
    for copy in four:
        copy.wait()
    total_a = s3a[x].astype(F32) + r4a[...].astype(F32)
    total_b = s3b[x].astype(F32) + r4b[...].astype(F32)
    root = jnp.sqrt((counts[2] + rcounts[7])[0:1, 0:1])
    local.wait()
    early[0].wait()
    here = (block // 16) == waves
    filters = jnp.where(here, mine[...], theirs[...])
    all_ref[core, y, z, x, :, 0:CHUNK] = (
        filters[:, 0:CHUNK] * (total_a.T / root)
    ).astype(BF)
    all_ref[core, y, z, x, :, CHUNK:PART] = (
        filters[:, CHUNK:PART] * (total_b.T / root)
    ).astype(BF)

    own = all_ref.at[core, y, z, x]
    remote(own, own, along_x()).wait()
    steps = []
    lane_a, lane_b = pl.ds(0, CHUNK), pl.ds(CHUNK, CHUNK)
    for d in (1, 2, 3):
        piece = all_ref.at[core, y, z, :, :, lane_a]
        steps.append(remote(piece, piece, along_z(d)))
        piece = all_ref.at[core, y, z, :, :, lane_b]
        steps.append(remote(piece, piece, along_y(d)))
    for copy in steps:
        copy.wait()
    steps = []
    for d in (1, 2, 3):
        piece = all_ref.at[core, y, :, :, :, lane_a]
        steps.append(remote(piece, piece, along_y(d)))
        piece = all_ref.at[core, :, z, :, :, lane_b]
        steps.append(remote(piece, piece, along_z(d)))
    for copy in steps:
        copy.wait()
    piece = all_ref.at[core]
    remote(piece, piece, sibling()).wait()
    for copy in early[1:]:
        copy.wait()


def exchange(sums, filters, feats, pos8, count, in_weight, out_weight):
    vmem = pl.BlockSpec(memory_space=pltpu.VMEM)
    hbm = pl.BlockSpec(memory_space=pl.ANY)
    return pl.pallas_call(
        exchange_kernel,
        in_specs=[vmem, hbm, hbm, hbm, vmem, hbm, hbm],
        out_specs=[vmem, hbm, hbm, hbm, hbm],
        out_shape=(
            jax.ShapeDtypeStruct((2, 4, 4, 2, CHUNK, PART), BF),
            jax.ShapeDtypeStruct(in_weight.shape, BF),
            jax.ShapeDtypeStruct(out_weight.shape, BF),
            jax.ShapeDtypeStruct((2, 2 * CAP, PART), BF),
            jax.ShapeDtypeStruct((2, 8, 2 * CAP), F32),
        ),
        scratch_shapes=[
            pltpu.VMEM((4, 4, 2, PART, CHUNK), BF),
            pltpu.VMEM((4, 4, 2, PART, CHUNK), BF),
            pltpu.VMEM((3, 4, 2, CHUNK, CHUNK), BF),
            pltpu.VMEM((3, 4, 2, CHUNK, CHUNK), BF),
            pltpu.VMEM((4, 2, CHUNK, CHUNK), BF),
            pltpu.VMEM((4, 2, CHUNK, CHUNK), BF),
            pltpu.VMEM((3, 2, CHUNK, CHUNK), BF),
            pltpu.VMEM((3, 2, CHUNK, CHUNK), BF),
            pltpu.VMEM((2, CHUNK, CHUNK), BF),
            pltpu.VMEM((2, CHUNK, CHUNK), BF),
            pltpu.VMEM((CHUNK, CHUNK), BF),
            pltpu.VMEM((CHUNK, CHUNK), BF),
            pltpu.VMEM((CHUNK, PART), F32),
            pltpu.VMEM((CHUNK, PART), F32),
            pltpu.VMEM((3, 8, 128), F32),
            pltpu.VMEM((8, 8, 128), F32),
            pltpu.SemaphoreType.DMA((48,)),
            pltpu.SemaphoreType.DMA((48,)),
            pltpu.SemaphoreType.DMA,
        ],
        compiler_params=params(collective_id=0, has_side_effects=True),
    )(sums, filters, feats, pos8, count, in_weight, out_weight)


def merge_kernel(
    neigh_ref, fall_ref, cos_ref, sin_ref, all_ref, feats_ref, wide_ref, widepos_ref,
    column_ref, mix_ref, merged_ref,
):
    far = jnp.dot(cos_ref[...], all_ref[0:K, :], preferred_element_type=F32)
    far += jnp.dot(sin_ref[...], all_ref[K:, :], preferred_element_type=F32)
    base = feats_ref[...].astype(F32) + far * (1.0 / math.sqrt(K))
    step = pl.program_id(0)
    for c in range(TILE // CAP):
        cell = step * (TILE // CAP) + c
        rows = slice(c * CAP, (c + 1) * CAP)
        here = [column_ref[rows, p : p + 1] for p in range(3)]
        sums = [jnp.zeros((CAP, PART), F32) for _ in range(G)]
        for n in range(NB):
            partner = cell + HW + neigh_ref[cell * NB + n]
            lanes = pl.ds(pl.multiple_of(partner * CAP, CAP), CAP)
            there = widepos_ref[:, lanes]
            feats = wide_ref[lanes, :]
            squared = jnp.zeros((CAP, CAP), F32)
            for p in range(3):
                d = here[p] - there[p : p + 1, :]
                squared += d * d
            for g in range(G):
                weight = jnp.exp(-fall_ref[g] * squared).astype(BF)
                sums[g] += jnp.dot(weight, feats, preferred_element_type=F32)
        near = jnp.zeros((CAP, PART), F32)
        for g in range(G):
            near += sums[g] * mix_ref[g : g + 1, :]
        merged_ref[rows, :] = base[rows, :] + near


def merge(neigh, fall, cosine, sine, filtered, feats, wide, widepos, column, mix):
    once = pl.Buffered(1)
    return pl.pallas_call(
        merge_kernel,
        grid=(ROWS // TILE,),
        in_specs=[
            pl.BlockSpec(memory_space=pltpu.SMEM),
            pl.BlockSpec(memory_space=pltpu.SMEM),
            pl.BlockSpec((TILE, K), lambda i: (i, 0)),
            pl.BlockSpec((TILE, K), lambda i: (i, 0)),
            pl.BlockSpec((2 * K, PART), lambda i: (0, 0), pipeline_mode=once),
            pl.BlockSpec((TILE, PART), lambda i: (i, 0)),
            pl.BlockSpec((ROWS + 4 * CAP, PART), lambda i: (0, 0)),
            pl.BlockSpec((8, ROWS + 4 * CAP), lambda i: (0, 0)),
            pl.BlockSpec((TILE, 3), lambda i: (i, 0)),
            pl.BlockSpec((G, PART), lambda i: (0, 0)),
        ],
        out_specs=pl.BlockSpec((TILE, PART), lambda i: (i, 0)),
        out_shape=jax.ShapeDtypeStruct((ROWS, PART), F32),
        compiler_params=params(),
    )(neigh, fall, cosine, sine, filtered, feats, wide, widepos, column, mix)


PIECES = 4
PIECE = HALF // PIECES


def mlp_kernel(
    merged_ref, gain_ref, in_ref, in2_ref, out_ref, out2_ref, result_ref,
    outgoing, incoming, back, returned, send_sem, recv_sem,
):
    waves = lax.axis_index("waves")
    other = 1 - waves
    partner = {"cells": lax.axis_index("cells"), "waves": other}
    barrier = pltpu.get_barrier_semaphore()
    pl.semaphore_signal(barrier, inc=1, device_id=partner, device_id_type=MESH)
    pl.semaphore_wait(barrier, 1)

    def remote(src, dst, n):
        copy = pltpu.make_async_remote_copy(
            src_ref=src, dst_ref=dst, send_sem=send_sem.at[n], recv_sem=recv_sem.at[n],
            device_id=partner, device_id_type=MESH,
        )
        copy.start()
        return copy

    own = pl.multiple_of(waves * PART, PART)
    far = pl.multiple_of(other * PART, PART)
    there = []
    for q in range(PIECES):
        rows = pl.ds(pl.multiple_of(other * HALF + q * PIECE, PIECE), PIECE)
        outgoing[q] = merged_ref[rows, :].astype(BF)
        there.append(remote(outgoing.at[q], incoming.at[q], q))
    returns = []
    for q in range(PIECES):
        there[q].wait()
        rows = pl.ds(pl.multiple_of(waves * HALF + q * PIECE, PIECE), PIECE)
        mine = merged_ref[rows, :]
        theirs = incoming[q].astype(F32)
        square = jnp.sum(mine * mine + theirs * theirs, axis=1, keepdims=True)
        scale = lax.rsqrt(square * (1.0 / F) + EPS)
        mine_n = (mine * scale * gain_ref[:, pl.ds(own, PART)]).astype(BF)
        theirs_n = (theirs * scale * gain_ref[:, pl.ds(far, PART)]).astype(BF)
        add_mine, add_theirs = mine, jnp.zeros_like(mine)
        for first, second in ((in_ref, out_ref), (in2_ref, out2_ref)):
            hidden = jnp.dot(
                mine_n, first[pl.ds(own, PART), :], preferred_element_type=F32
            ) + jnp.dot(theirs_n, first[pl.ds(far, PART), :], preferred_element_type=F32)
            hidden = (hidden / (1.0 + jnp.exp(-hidden))).astype(BF)
            add_mine += jnp.dot(
                hidden, second[:, pl.ds(own, PART)], preferred_element_type=F32
            )
            add_theirs += jnp.dot(
                hidden, second[:, pl.ds(far, PART)], preferred_element_type=F32
            )
        back[q] = add_theirs.astype(BF)
        returns.append(remote(back.at[q], returned.at[q], PIECES + q))
        result_ref[rows, :] = add_mine.astype(BF)
    for q in range(PIECES):
        returns[q].wait()
        rows = pl.ds(pl.multiple_of(other * HALF + q * PIECE, PIECE), PIECE)
        result_ref[rows, :] = (merged_ref[rows, :] + returned[q].astype(F32)).astype(BF)


def mlp(merged, gain, in_weight, in2, out_weight, out2):
    vmem = pl.BlockSpec(memory_space=pltpu.VMEM)
    return pl.pallas_call(
        mlp_kernel,
        in_specs=[vmem] * 6,
        out_specs=vmem,
        out_shape=jax.ShapeDtypeStruct((ROWS, PART), BF),
        scratch_shapes=[pltpu.VMEM((PIECES, PIECE, PART), BF)] * 4
        + [pltpu.SemaphoreType.DMA((2 * PIECES,))] * 2,
        compiler_params=params(collective_id=1, has_side_effects=True),
    )(merged, gain, in_weight, in2, out_weight, out2)


def shards(
    features, positions, occupancy, neighbours, wavevectors, filters,
    falloffs, mixing, norm_gain, in_weight, out_weight,
):
    cells = lax.axis_index("cells")
    waves = lax.axis_index("waves")
    is_live = (
        jnp.arange(CAP, dtype=jnp.int32)[None, :] < occupancy[:, None]
    ).reshape(ROWS, 1)
    masked = jnp.where(is_live, features, jnp.zeros_like(features))
    whole_waves = lax.all_gather(wavevectors, "waves", axis=1, tiled=True)
    left, right = phase_operands(positions, whole_waves)
    cosine, sine, sums = forward(left, right, masked.T)
    pos8 = jnp.pad(positions, ((0, 5), (0, 0)))
    count = jnp.full((8, 128), jnp.sum(occupancy).astype(F32))
    filtered, in2, out2, edges, edge_pos = exchange(
        sums.reshape(2, 4, 4, 2, PART, CHUNK), filters, masked, pos8, count,
        in_weight, out_weight,
    )
    length = jnp.float32(LENGTH)
    shift_low = jnp.where(cells == 0, -length, 0.0)
    shift_high = jnp.where(cells == 63, length, 0.0)
    first = jnp.zeros((8, 1), F32).at[0].set(1.0)
    widepos = jnp.concatenate(
        [edge_pos[0] + first * shift_low, pos8, edge_pos[1] + first * shift_high], axis=1
    )
    wide = jnp.concatenate([edges[0], masked, edges[1]], axis=0)
    mix = lax.dynamic_slice_in_dim(mixing, waves * PART, PART, 1)
    merged = merge(
        neighbours.reshape(LOCAL * NB), falloffs, cosine, sine,
        filtered.reshape(2 * K, PART), features, wide, widepos, positions.T, mix,
    )
    return mlp(merged, norm_gain[None, :], in_weight, in2, out_weight, out2)


def solution(mesh):
    placed = (
        P("cells", "waves"),
        P(None, "cells"),
        P("cells"),
        P("cells", None),
        P(None, "waves"),
        P("waves", None),
        P(),
        P(),
        P(),
        P(None, "waves"),
        P("waves", None),
    )
    return jax.shard_map(
        shards, mesh=mesh, in_specs=placed, out_specs=P("cells", "waves"), check_vma=False
    )
```

```python
import functools
import math

import jax
import jax.numpy as jnp
from jax import lax
from jax.experimental import pallas as pl
from jax.experimental.pallas import tpu as pltpu
from jax.sharding import PartitionSpec as P

F = 512
K = 4096
CAP = 128
HW = 2
NB = 3
G = 4
EPS = 1e-06
WAVES = 2
PART = 256
ROWS = 2048
LOCAL = 16
LENGTH = 1024.0
KP = 64
TILE = 512
TILES = K // TILE
QUARTERS = 4
BLOCK = 32
LANES = 128
HALF = ROWS // 2
BF = jnp.bfloat16
F32 = jnp.float32
MESH = pl.DeviceIdType.MESH
TURN = 1.0 / (2.0 * math.pi)
LOG2E = 1.4426950408889634

SIN = (4.442867900911655, -7.307443330487869, 3.594787161239145, -0.784371485095076)
COS = (1.4142040799995839, -6.977641979004694, 5.715237169770743, -1.7283443233022544)


def params(**more):
    return pltpu.CompilerParams(vmem_limit_bytes=62 << 20, **more)


def split3(v):
    a = v.astype(BF).astype(F32)
    b = (v - a).astype(BF).astype(F32)
    c = ((v - a) - b).astype(BF).astype(F32)
    return a, b, c


def nearest(v):
    return lax.round(v, lax.RoundingMethod.TO_NEAREST_EVEN)


def trig(turns):
    r = turns - nearest(turns)
    s = r * r
    half_sin = r * (SIN[0] + s * (SIN[1] + s * (SIN[2] + s * SIN[3])))
    half_cos = COS[0] + s * (COS[1] + s * (COS[2] + s * COS[3]))
    return (1.0 - half_sin * half_sin).astype(BF), (half_sin * half_cos).astype(BF)


def pieces_of(parts, width):
    row = lax.broadcasted_iota(jnp.int32, (16, width), 0)
    out = jnp.zeros((16, width), F32)
    for n, piece in enumerate(parts):
        out = jnp.where(row == n, jnp.broadcast_to(piece, (16, width)), out)
    return out


def cell_index(z, x, y, core):
    return ((z * 2 + x) * 4 + y) * 2 + core


MESSAGES = 29
COUNTS = 8
PIECES = 4
PIECE = HALF // PIECES


def layer(
    occ_ref, neigh_ref, fall_ref,
    feats_ref, pos_ref, wave_ref, mix_ref, gain_ref, in_ref, out_ref, filt_ref,
    result_ref,
    wide, widepos, waves_all, left, right, cosines, sines, sums,
    r1, r2a, r2b, s2a, s2b, r3a, r3b, s3a, s3b, r4a, r4b, filtered,
    mine, theirs, counts, rcounts, merged, in2, out2,
    outgoing, incoming, back, returned,
    send_sem, recv_sem, csend_sem, crecv_sem, esend_sem, erecv_sem, msend_sem, mrecv_sem,
    local_sem,
):
    cells = lax.axis_index("cells")
    waves = lax.axis_index("waves")
    other = 1 - waves
    z, x, y, core = cells // 16, (cells // 8) % 2, (cells // 2) % 4, cells % 2

    def at(cell):
        return {"cells": cell, "waves": waves}

    def along_y(d):
        return at(cell_index(z, x, lax.rem(y + d, 4), core))

    def along_z(d):
        return at(cell_index(lax.rem(z + d, 4), x, y, core))

    sibling = at(cell_index(z, x, y, 1 - core))
    along_x = at(cell_index(z, 1 - x, y, core))
    above = at(lax.rem(cells + 1, 64))
    below = at(lax.rem(cells + 63, 64))
    partner = {"cells": cells, "waves": other}

    def copy_of(src, dst, sends, receives, n, device):
        return pltpu.make_async_remote_copy(
            src_ref=src, dst_ref=dst, send_sem=sends.at[n], recv_sem=receives.at[n],
            device_id=device, device_id_type=MESH,
        )

    barrier = pltpu.get_barrier_semaphore()
    peers = [sibling, along_x, partner, above, below]
    peers += [along_y(d) for d in (1, 2, 3)] + [along_z(d) for d in (1, 2, 3)]
    for peer in peers:
        pl.semaphore_signal(barrier, inc=1, device_id=peer, device_id_type=MESH)

    for t in range(TILES // 2):
        waves_all[waves * (TILES // 2) + t, 0:3, :] = wave_ref[:, t * TILE : (t + 1) * TILE]
    for c in range(LOCAL):
        widepos[c + HW, 0:3, :] = pos_ref[:, c * CAP : (c + 1) * CAP]
    slot = lax.broadcasted_iota(jnp.int32, (CAP, PART), 0)
    total = jnp.float32(0.0)
    for c in range(LOCAL):
        block = feats_ref[c * CAP : (c + 1) * CAP, :]
        wide[c + HW] = jnp.where(slot < occ_ref[c], block.astype(F32), 0.0).astype(BF)
        total = total + occ_ref[c].astype(F32)
    counts[0] = jnp.full((8, LANES), total)
    pl.semaphore_wait(barrier, len(peers))

    index = y * 8 + z * 2 + x
    own_lanes = pl.ds(pl.multiple_of(waves * PART, PART), PART)
    far_lanes = pl.ds(pl.multiple_of(other * PART, PART), PART)

    def filter_rows(half):
        return pl.ds(pl.multiple_of(half * 1024 + index * BLOCK, BLOCK), BLOCK)

    own_tiles = pl.ds(waves * (TILES // 2), TILES // 2)
    early = [
        (waves_all.at[own_tiles], waves_all.at[own_tiles], partner),
        (filt_ref.at[filter_rows(0), far_lanes], theirs.at[0], partner),
        (filt_ref.at[filter_rows(1), far_lanes], theirs.at[1], partner),
        (widepos.at[pl.ds(HW, HW)], widepos.at[pl.ds(LOCAL + HW, HW)], below),
        (widepos.at[pl.ds(LOCAL, HW)], widepos.at[pl.ds(0, HW)], above),
        (wide.at[pl.ds(HW, HW)], wide.at[pl.ds(LOCAL + HW, HW)], below),
        (wide.at[pl.ds(LOCAL, HW)], wide.at[pl.ds(0, HW)], above),
        (in_ref, in2, partner),
        (out_ref, out2, partner),
    ]
    early = [
        copy_of(src, dst, esend_sem, erecv_sem, n, device)
        for n, (src, dst, device) in enumerate(early)
    ]
    for copy in early:
        copy.start()
    locals_ = [
        pltpu.make_async_copy(
            filt_ref.at[filter_rows(h), own_lanes], mine.at[h], local_sem.at[h]
        )
        for h in range(2)
    ]
    for copy in locals_:
        copy.start()

    first = cells * LOCAL
    cell_of = lax.broadcasted_iota(jnp.int32, (1, ROWS), 1) // CAP
    parts = []
    for p in range(3):
        v = pos_ref[p : p + 1, :]
        if p == 0:
            v = v - (cell_of + first).astype(F32)
        a, b, _ = split3(v)
        parts += [a, a, b, b]
    row = lax.broadcasted_iota(jnp.int32, (16, ROWS), 0)
    hot = (row == lax.broadcasted_iota(jnp.int32, (16, ROWS), 1) // CAP).astype(F32)
    left[...] = jnp.concatenate([pieces_of(parts, ROWS), hot, hot, hot], axis=0).T.astype(BF)
    merged[...] = feats_ref[...].astype(F32)
    early[0].wait()

    def tile(i):
        waves_here = waves_all[i]
        parts = []
        for p in range(3):
            k1, k2, _ = split3(waves_here[p : p + 1, :] * TURN)
            parts += [k1, k2, k1, k2]
        cell = (lax.broadcasted_iota(jnp.int32, (16, TILE), 0) + first).astype(F32)
        whole = cell * (waves_here[0:1, :] * TURN)
        whole = whole - nearest(whole)
        right[...] = jnp.concatenate([pieces_of(parts, TILE), *split3(whole)], axis=0).astype(BF)
        for b in range(ROWS // 512):
            rows = slice(b * 512, (b + 1) * 512)
            turns = jnp.dot(left[rows, :], right[...], preferred_element_type=F32)
            cosine, sine = trig(turns)
            cosines[i, rows, :] = cosine
            sines[i, rows, :] = sine
        atoms = wide[HW : HW + LOCAL].reshape(ROWS, PART)
        q, p = i // 2, i % 2
        for n, held in enumerate((cosines, sines)):
            part = lax.dot_general(
                held[i], atoms, (((0,), (0,)), ((), ())), preferred_element_type=F32
            )
            sums[n, q, pl.ds(2 * p, 2)] = part.astype(BF).reshape(2, 4, 2, BLOCK, PART)

    lane_a, lane_b = pl.ds(0, LANES), pl.ds(LANES, LANES)

    def messages(stage, q):
        base = q * MESSAGES
        out = []

        def add(src, dst, n, device):
            out.append(copy_of(src, dst, send_sem, recv_sem, base + n, device))

        if stage == 1:
            add(sums.at[1 - core, q], r1.at[q], 0, sibling)
        elif stage == 4:
            add(s3a.at[q, 1 - x], r4a.at[q], 13, along_x)
            add(s3b.at[q, 1 - x], r4b.at[q], 14, along_x)
        elif stage == 5:
            piece = filtered.at[core, q, y, z, x]
            add(piece, piece, 15, along_x)
        elif stage == 8:
            piece = filtered.at[core, q]
            add(piece, piece, 28, sibling)
        else:
            for d in (1, 2, 3):
                ty, tz, m = lax.rem(y + d, 4), lax.rem(z + d, 4), d - 1
                if stage == 2:
                    add(sums.at[core, q, ty, :, :, :, lane_a], r2a.at[q, m], 1 + m, along_y(d))
                    add(sums.at[core, q, :, tz, :, :, lane_b], r2b.at[q, m], 4 + m, along_z(d))
                elif stage == 3:
                    add(s2a.at[q, tz], r3a.at[q, m], 7 + m, along_z(d))
                    add(s2b.at[q, ty], r3b.at[q, m], 10 + m, along_y(d))
                elif stage == 6:
                    piece = filtered.at[core, q, y, z, :, :, lane_a]
                    add(piece, piece, 16 + m, along_z(d))
                    piece = filtered.at[core, q, y, z, :, :, lane_b]
                    add(piece, piece, 19 + m, along_y(d))
                elif stage == 7:
                    piece = filtered.at[core, q, y, :, :, :, lane_a]
                    add(piece, piece, 22 + m, along_y(d))
                    piece = filtered.at[core, q, :, z, :, :, lane_b]
                    add(piece, piece, 25 + m, along_z(d))
        return out

    def count_messages(stage):
        def make(src, n, device):
            return copy_of(counts.at[src], rcounts.at[n], csend_sem, crecv_sem, n, device)

        if stage == 1:
            return [make(0, 0, sibling)]
        if stage == 2:
            return [make(1, d, along_y(d)) for d in (1, 2, 3)]
        if stage == 3:
            return [make(2, 3 + d, along_z(d)) for d in (1, 2, 3)]
        return [make(3, 7, along_x)]

    def count_step(stage):
        if stage > 1:
            arrived = count_messages(stage - 1)
            for copy in arrived:
                copy.wait()
            begin = (0, 0, 1, 4, 7)[stage - 1]
            value = counts[stage - 2]
            for n in range(len(arrived)):
                value = value + rcounts[begin + n]
            counts[stage - 1] = value
        if stage < 5:
            for copy in count_messages(stage):
                copy.start()

    def advance(stage, q):
        if stage > 1:
            for copy in messages(stage - 1, q):
                copy.wait()
        if stage <= 5:

            @pl.when(q == 0)
            def _():
                count_step(stage)
                if stage == 5:
                    for copy in early[1:3]:
                        copy.wait()
                    for copy in locals_:
                        copy.wait()

        if stage == 2:

            def add1(n, carry):
                yy, zz = n // 4, n % 4
                sums[core, q, yy, zz] = (
                    sums[core, q, yy, zz].astype(F32) + r1[q, yy, zz].astype(F32)
                ).astype(BF)
                return carry

            lax.fori_loop(0, 16, add1, 0)
        elif stage == 3:
            for p in range(4):
                a = sums[core, q, y, p, :, :, 0:LANES].astype(F32)
                b = sums[core, q, p, z, :, :, LANES:PART].astype(F32)
                for d in range(3):
                    a += r2a[q, d, p].astype(F32)
                    b += r2b[q, d, p].astype(F32)
                s2a[q, p] = a.astype(BF)
                s2b[q, p] = b.astype(BF)
        elif stage == 4:
            a, b = s2a[q, z].astype(F32), s2b[q, y].astype(F32)
            for d in range(3):
                a += r3a[q, d].astype(F32)
                b += r3b[q, d].astype(F32)
            s3a[q] = a.astype(BF)
            s3b[q] = b.astype(BF)
        elif stage == 5:
            root = jnp.sqrt(counts[4][0:1, :])
            here = (q // 2) == waves
            filters = jnp.where(here, mine[q % 2], theirs[q % 2])
            a = s3a[q, x].astype(F32) + r4a[q].astype(F32)
            b = s3b[q, x].astype(F32) + r4b[q].astype(F32)
            filtered[core, q, y, z, x, :, 0:LANES] = (
                filters[:, 0:LANES] * (a / root)
            ).astype(BF)
            filtered[core, q, y, z, x, :, LANES:PART] = (
                filters[:, LANES:PART] * (b / root)
            ).astype(BF)
        if stage < 9:
            for copy in messages(stage, q):
                copy.start()

    def near(c):
        here = widepos[c + HW].T
        sums_ = [jnp.zeros((CAP, PART), F32) for _ in range(G)]
        for n in range(NB):
            place = c + HW + neigh_ref[c * NB + n]
            shift = jnp.where((cells == 0) & (place < HW), -LENGTH, 0.0) + jnp.where(
                (cells == 63) & (place >= LOCAL + HW), LENGTH, 0.0
            )
            there = widepos[place]
            squared = None
            for p in range(3):
                d = here[:, p : p + 1] - (there[p : p + 1, :] + (shift if p == 0 else 0.0))
                squared = d * d if squared is None else squared + d * d
            block = wide[place]
            for g in range(G):
                weight = jnp.exp(-fall_ref[g] * squared).astype(BF)
                sums_[g] += jnp.dot(weight, block, preferred_element_type=F32)
        rows = pl.ds(pl.multiple_of(c * CAP, CAP), CAP)
        value = merged[rows, :]
        for g in range(G):
            value += sums_[g] * mix_ref[g : g + 1, own_lanes]
        merged[rows, :] = value

    scale_far = 1.0 / math.sqrt(K)

    def far(q, rows):
        value = None
        for n, held in enumerate((cosines, sines)):
            factors = filtered[n, q].reshape(2 * TILE, PART)
            for p in range(2):
                term = jnp.dot(
                    held[2 * q + p, rows, :],
                    factors[p * TILE : (p + 1) * TILE],
                    preferred_element_type=F32,
                )
                value = term if value is None else value + term
        return merged[rows, :] + value * scale_far

    def far_block(q, b):
        rows = pl.ds(pl.multiple_of(b * PIECE, PIECE), PIECE)
        merged[rows, :] = far(q, rows)

    def slots(m, carry):
        @pl.when(m < 4)
        def _():
            tile(2 * m)

        @pl.when(m == 4)
        def _():
            for copy in early[3:7]:
                copy.wait()

        @pl.when(m >= 4)
        def _():
            lax.fori_loop(0, 2, lambda j, c: (near((m - 4) * 4 + j), c)[1], 0)

        for stage in (2, 4, 6, 8):
            q = m - stage // 2

            @pl.when((q >= 0) & (q < QUARTERS))
            def _(stage=stage, q=q):
                advance(stage, q)

        @pl.when(m < 4)
        def _():
            tile(2 * m + 1)
            advance(1, m)

        @pl.when(m >= 4)
        def _():
            lax.fori_loop(2, 4, lambda j, c: (near((m - 4) * 4 + j), c)[1], 0)

        for stage in (3, 5, 7, 9):
            q = m - (stage - 1) // 2

            @pl.when((q >= 0) & (q < QUARTERS))
            def _(stage=stage, q=q):
                advance(stage, q)

        @pl.when((m >= 4) & (m < 7))
        def _():
            lax.fori_loop(0, ROWS // PIECE, lambda b, c: (far_block(m - 4, b), c)[1], 0)

        return carry

    lax.fori_loop(0, 8, slots, 0)

    def forth(n):
        return copy_of(outgoing.at[n], incoming.at[n], msend_sem, mrecv_sem, n, partner)

    def home(n):
        return copy_of(back.at[n], returned.at[n], msend_sem, mrecv_sem, PIECES + n, partner)

    def rows_of(side, n):
        return pl.ds(pl.multiple_of(side * HALF + n * PIECE, PIECE), PIECE)

    def give(n, carry):
        rows = rows_of(other, n)
        value = far(QUARTERS - 1, rows)
        merged[rows, :] = value
        outgoing[n] = value.astype(BF)
        forth(n).start()
        return carry

    def keep(n, carry):
        rows = rows_of(waves, n)
        merged[rows, :] = far(QUARTERS - 1, rows)
        return carry

    def mlp(n, carry):
        forth(n).wait()
        rows = rows_of(waves, n)
        own = merged[rows, :]
        their = incoming[n].astype(F32)
        square = jnp.sum(own * own + their * their, axis=1, keepdims=True)
        scale = lax.rsqrt(square * (1.0 / F) + EPS)
        own_n = (own * scale * gain_ref[:, own_lanes]).astype(BF)
        their_n = (their * scale * gain_ref[:, far_lanes]).astype(BF)
        add_own, add_their = own, jnp.zeros_like(own)
        for up, down in ((in_ref, out_ref), (in2, out2)):
            hidden = jnp.dot(
                own_n, up[own_lanes, :], preferred_element_type=F32
            ) + jnp.dot(their_n, up[far_lanes, :], preferred_element_type=F32)
            hidden = (hidden / (1.0 + jnp.exp(-hidden))).astype(BF)
            add_own += jnp.dot(hidden, down[:, own_lanes], preferred_element_type=F32)
            add_their += jnp.dot(hidden, down[:, far_lanes], preferred_element_type=F32)
        back[n] = add_their.astype(BF)
        home(n).start()
        result_ref[rows, :] = add_own.astype(BF)
        return carry

    def finish(n, carry):
        home(n).wait()
        rows = rows_of(other, n)
        result_ref[rows, :] = (merged[rows, :] + returned[n].astype(F32)).astype(BF)
        return carry

    lax.fori_loop(0, PIECES, give, 0)
    lax.fori_loop(0, PIECES, keep, 0)
    for copy in early[7:]:
        copy.wait()
    lax.fori_loop(0, PIECES, mlp, 0)
    lax.fori_loop(0, PIECES, finish, 0)


def shards(
    features, positions, occupancy, neighbours, wavevectors, filters,
    falloffs, mixing, norm_gain, in_weight, out_weight,
):
    smem = pl.BlockSpec(memory_space=pltpu.SMEM)
    vmem = pl.BlockSpec(memory_space=pltpu.VMEM)
    hbm = pl.BlockSpec(memory_space=pl.ANY)
    half = (QUARTERS, 3, 4, 2, BLOCK, LANES)
    return pl.pallas_call(
        layer,
        in_specs=[smem] * 3 + [vmem] * 7 + [hbm],
        out_specs=vmem,
        out_shape=jax.ShapeDtypeStruct((ROWS, PART), BF),
        scratch_shapes=[
            pltpu.VMEM((LOCAL + 2 * HW, CAP, PART), BF),
            pltpu.VMEM((LOCAL + 2 * HW, 8, CAP), F32),
            pltpu.VMEM((TILES, 8, TILE), F32),
            pltpu.VMEM((ROWS, KP), BF),
            pltpu.VMEM((KP, TILE), BF),
            pltpu.VMEM((TILES, ROWS, TILE), BF),
            pltpu.VMEM((TILES, ROWS, TILE), BF),
            pltpu.VMEM((2, QUARTERS, 4, 4, 2, BLOCK, PART), BF),
            pltpu.VMEM((QUARTERS, 4, 4, 2, BLOCK, PART), BF),
            pltpu.VMEM(half, BF),
            pltpu.VMEM(half, BF),
            pltpu.VMEM((QUARTERS, 4, 2, BLOCK, LANES), BF),
            pltpu.VMEM((QUARTERS, 4, 2, BLOCK, LANES), BF),
            pltpu.VMEM((QUARTERS, 3, 2, BLOCK, LANES), BF),
            pltpu.VMEM((QUARTERS, 3, 2, BLOCK, LANES), BF),
            pltpu.VMEM((QUARTERS, 2, BLOCK, LANES), BF),
            pltpu.VMEM((QUARTERS, 2, BLOCK, LANES), BF),
            pltpu.VMEM((QUARTERS, BLOCK, LANES), BF),
            pltpu.VMEM((QUARTERS, BLOCK, LANES), BF),
            pltpu.VMEM((2, QUARTERS, 4, 4, 2, BLOCK, PART), BF),
            pltpu.VMEM((2, BLOCK, PART), F32),
            pltpu.VMEM((2, BLOCK, PART), F32),
            pltpu.VMEM((5, 8, LANES), F32),
            pltpu.VMEM((COUNTS, 8, LANES), F32),
            pltpu.VMEM((ROWS, PART), F32),
            pltpu.VMEM(in_weight.shape, BF),
            pltpu.VMEM(out_weight.shape, BF),
        ]
        + [pltpu.VMEM((PIECES, PIECE, PART), BF)] * 4
        + [pltpu.SemaphoreType.DMA((QUARTERS * MESSAGES,))] * 2
        + [pltpu.SemaphoreType.DMA((COUNTS,))] * 2
        + [pltpu.SemaphoreType.DMA((9,))] * 2
        + [pltpu.SemaphoreType.DMA((2 * PIECES,))] * 2
        + [pltpu.SemaphoreType.DMA((2,))],
        compiler_params=params(collective_id=0, has_side_effects=True),
    )(
        occupancy, neighbours.reshape(LOCAL * NB), falloffs,
        features, positions, wavevectors, mixing, norm_gain[None, :],
        in_weight, out_weight, filters,
    )


def solution(mesh):
    placed = (
        P("cells", "waves"),
        P(None, "cells"),
        P("cells"),
        P("cells", None),
        P(None, "waves"),
        P("waves", None),
        P(),
        P(),
        P(),
        P(None, "waves"),
        P("waves", None),
    )
    return jax.shard_map(
        shards, mesh=mesh, in_specs=placed, out_specs=P("cells", "waves"), check_vma=False
    )
```

```python
import functools
import math

import jax
import jax.numpy as jnp
from jax import lax
from jax.experimental import pallas as pl
from jax.experimental.pallas import tpu as pltpu
from jax.sharding import PartitionSpec as P

F = 512
K = 4096
CAP = 128
HW = 2
NB = 3
G = 4
EPS = 1e-06
WAVES = 2
PART = 256
ROWS = 2048
LOCAL = 16
LENGTH = 1024.0
KP = 64
TILE = 512
TILES = K // TILE
QUARTERS = 4
BLOCK = 32
LANES = 128
HALF = ROWS // 2
BF = jnp.bfloat16
F32 = jnp.float32
MESH = pl.DeviceIdType.MESH
TURN = 1.0 / (2.0 * math.pi)
LOG2E = 1.4426950408889634

SIN = (4.442867900911655, -7.307443330487869, 3.594787161239145, -0.784371485095076)
COS = (1.4142040799995839, -6.977641979004694, 5.715237169770743, -1.7283443233022544)


def params(**more):
    return pltpu.CompilerParams(vmem_limit_bytes=62 << 20, **more)


def split3(v):
    a = v.astype(BF).astype(F32)
    b = (v - a).astype(BF).astype(F32)
    c = ((v - a) - b).astype(BF).astype(F32)
    return a, b, c


def nearest(v):
    return lax.round(v, lax.RoundingMethod.TO_NEAREST_EVEN)


def trig(turns):
    r = turns - nearest(turns)
    s = r * r
    half_sin = r * (SIN[0] + s * (SIN[1] + s * (SIN[2] + s * SIN[3])))
    half_cos = COS[0] + s * (COS[1] + s * (COS[2] + s * COS[3]))
    return (1.0 - half_sin * half_sin).astype(BF), (half_sin * half_cos).astype(BF)


def pieces_of(parts, width):
    row = lax.broadcasted_iota(jnp.int32, (16, width), 0)
    out = jnp.zeros((16, width), F32)
    for n, piece in enumerate(parts):
        out = jnp.where(row == n, jnp.broadcast_to(piece, (16, width)), out)
    return out


def cell_index(z, x, y, core):
    return ((z * 2 + x) * 4 + y) * 2 + core


MESSAGES = 10
COUNTS = 11
STAGES = 7
PIECES = 4
PIECE = HALF // PIECES


def layer(
    occ_ref, neigh_ref, fall_ref,
    feats_ref, pos_ref, wave_ref, mix_ref, gain_ref, in_ref, out_ref, filt_ref,
    result_ref,
    wide, widepos, waves_all, left, right, cosines, sines, sums,
    r1, r2a, r2b, s2a, s2b, r3a, r3b, filtered,
    mine, theirs, counts, rcounts, merged, weights,
    outgoing, incoming, back, returned,
    send_sem, recv_sem, csend_sem, crecv_sem, esend_sem, erecv_sem, msend_sem, mrecv_sem,
    wsend_sem, wrecv_sem, local_sem,
):
    cells = lax.axis_index("cells")
    waves = lax.axis_index("waves")
    other = 1 - waves
    z, x, y, core = cells // 16, (cells // 8) % 2, (cells // 2) % 4, cells % 2

    def at(cell):
        return {"cells": cell, "waves": waves}

    def along_y(d):
        return at(cell_index(z, x, lax.rem(y + d, 4), core))

    def along_z(d):
        return at(cell_index(lax.rem(z + d, 4), x, y, core))

    def among_zx(d):
        g = lax.rem(z * 2 + x + d, 8)
        return g // 2, g % 2, at(cell_index(g // 2, g % 2, y, core))

    def among_yx(d):
        g = lax.rem(y * 2 + x + d, 8)
        return g // 2, g % 2, at(cell_index(z, g % 2, g // 2, core))

    sibling = at(cell_index(z, x, y, 1 - core))
    above = at(lax.rem(cells + 1, 64))
    below = at(lax.rem(cells + 63, 64))
    partner = {"cells": cells, "waves": other}

    def copy_of(src, dst, sends, receives, n, device):
        return pltpu.make_async_remote_copy(
            src_ref=src, dst_ref=dst, send_sem=sends.at[n], recv_sem=receives.at[n],
            device_id=device, device_id_type=MESH,
        )

    barrier = pltpu.get_barrier_semaphore()
    peers = [sibling, partner, above, below]
    peers += [among(d)[2] for d in range(1, 8) for among in (among_zx, among_yx)]
    for peer in peers:
        pl.semaphore_signal(barrier, inc=1, device_id=peer, device_id_type=MESH)

    for t in range(TILES // 2):
        waves_all[t, 0:3, :] = wave_ref[:, t * TILE : (t + 1) * TILE]
    for c in range(LOCAL):
        widepos[c + HW, 0:3, :] = pos_ref[:, c * CAP : (c + 1) * CAP]
    slot = lax.broadcasted_iota(jnp.int32, (CAP, PART), 0)
    total = jnp.float32(0.0)
    for c in range(LOCAL):
        block = feats_ref[c * CAP : (c + 1) * CAP, :]
        wide[c + HW] = jnp.where(slot < occ_ref[c], block.astype(F32), 0.0).astype(BF)
        total = total + occ_ref[c].astype(F32)
    counts[0] = jnp.full((8, LANES), total)

    index = y * 8 + z * 2 + x
    own_lanes = pl.ds(pl.multiple_of(waves * PART, PART), PART)
    far_lanes = pl.ds(pl.multiple_of(other * PART, PART), PART)

    def filter_rows(half):
        return pl.ds(pl.multiple_of(half * 1024 + index * BLOCK, BLOCK), BLOCK)

    own_tiles, far_tiles = pl.ds(0, TILES // 2), pl.ds(TILES // 2, TILES // 2)
    early = [
        (waves_all.at[own_tiles], waves_all.at[far_tiles], partner),
        (filt_ref.at[filter_rows(0), far_lanes], theirs.at[0], partner),
        (filt_ref.at[filter_rows(1), far_lanes], theirs.at[1], partner),
        (widepos.at[pl.ds(HW, HW)], widepos.at[pl.ds(LOCAL + HW, HW)], below),
        (widepos.at[pl.ds(LOCAL, HW)], widepos.at[pl.ds(0, HW)], above),
        (wide.at[pl.ds(HW, HW)], wide.at[pl.ds(LOCAL + HW, HW)], below),
        (wide.at[pl.ds(LOCAL, HW)], wide.at[pl.ds(0, HW)], above),
    ]
    early = [
        copy_of(src, dst, esend_sem, erecv_sem, n, device)
        for n, (src, dst, device) in enumerate(early)
    ]
    locals_ = [
        pltpu.make_async_copy(
            filt_ref.at[filter_rows(h), own_lanes], mine.at[h], local_sem.at[h]
        )
        for h in range(2)
    ]
    for copy in locals_:
        copy.start()

    first = cells * LOCAL
    cell_of = lax.broadcasted_iota(jnp.int32, (1, ROWS), 1) // CAP
    parts = []
    for p in range(3):
        v = pos_ref[p : p + 1, :]
        if p == 0:
            v = v - (cell_of + first).astype(F32)
        a, b, _ = split3(v)
        parts += [a, a, b, b]
    row = lax.broadcasted_iota(jnp.int32, (16, ROWS), 0)
    hot = (row == lax.broadcasted_iota(jnp.int32, (16, ROWS), 1) // CAP).astype(F32)
    left[...] = jnp.concatenate([pieces_of(parts, ROWS), hot, hot, hot], axis=0).T.astype(BF)
    merged[...] = feats_ref[...].astype(F32)

    def tile(i):
        waves_here = waves_all[i]
        parts = []
        for p in range(3):
            k1, k2, _ = split3(waves_here[p : p + 1, :] * TURN)
            parts += [k1, k2, k1, k2]
        cell = (lax.broadcasted_iota(jnp.int32, (16, TILE), 0) + first).astype(F32)
        whole = cell * (waves_here[0:1, :] * TURN)
        whole = whole - nearest(whole)
        right[...] = jnp.concatenate([pieces_of(parts, TILE), *split3(whole)], axis=0).astype(BF)
        for b in range(ROWS // 512):
            rows = slice(b * 512, (b + 1) * 512)
            turns = jnp.dot(left[rows, :], right[...], preferred_element_type=F32)
            cosine, sine = trig(turns)
            cosines[i, rows, :] = cosine
            sines[i, rows, :] = sine
        atoms = wide[HW : HW + LOCAL].reshape(ROWS, PART)
        q, p = i // 2, i % 2
        for n, held in enumerate((cosines, sines)):
            part = lax.dot_general(
                held[i], atoms, (((0,), (0,)), ((), ())), preferred_element_type=F32
            )
            sums[n, q, pl.ds(2 * p, 2)] = part.astype(BF).reshape(2, 4, 2, BLOCK, PART)

    lane_a, lane_b = pl.ds(0, LANES), pl.ds(LANES, LANES)

    def messages(stage, q):
        base = q * MESSAGES
        out = []

        def add(src, dst, n, device):
            out.append(copy_of(src, dst, send_sem, recv_sem, base + n, device))

        if stage == 1:
            add(sums.at[1 - core, q], r1.at[q], 0, sibling)
        elif stage == 6:
            piece = filtered.at[core, q]
            add(piece, piece, 1, sibling)
        elif stage in (2, 5):
            for d in (1, 2, 3):
                ty, tz, m = lax.rem(y + d, 4), lax.rem(z + d, 4), d - 1
                if stage == 2:
                    add(sums.at[core, q, ty, :, :, :, lane_a], r2a.at[q, m], 2, along_y(d))
                    add(sums.at[core, q, :, tz, :, :, lane_b], r2b.at[q, m], 3, along_z(d))
                else:
                    piece = filtered.at[core, q, y, :, :, :, lane_a]
                    add(piece, piece, 4, along_y(d))
                    piece = filtered.at[core, q, :, z, :, :, lane_b]
                    add(piece, piece, 5, along_z(d))
        else:
            for d in range(1, 8):
                m = d - 1
                if stage == 3:
                    tz, tx, device = among_zx(d)
                    add(s2a.at[q, tz, tx], r3a.at[q, m], 6, device)
                    ty, tx, device = among_yx(d)
                    add(s2b.at[q, ty, tx], r3b.at[q, m], 7, device)
                else:
                    piece = filtered.at[core, q, y, z, x, :, lane_a]
                    add(piece, piece, 8, among_zx(d)[2])
                    piece = filtered.at[core, q, y, z, x, :, lane_b]
                    add(piece, piece, 9, among_yx(d)[2])
        return out

    def arrivals(stage, q):
        if stage in (1, 6):
            return messages(stage, q)
        first, a, b = {2: (2, r2a, r2b), 3: (6, r3a, r3b), 4: (8, r3a, r3b), 5: (4, r2a, r2b)}[stage]
        return [
            copy_of(
                held.at[q], held.at[q], send_sem, recv_sem,
                q * MESSAGES + first + n, sibling,
            )
            for n, held in enumerate((a, b))
        ]

    def count_messages(stage):
        def make(src, n, device):
            return copy_of(counts.at[src], rcounts.at[n], csend_sem, crecv_sem, n, device)

        if stage == 1:
            return [make(0, 0, sibling)]
        if stage == 2:
            return [make(1, d, along_y(d)) for d in (1, 2, 3)]
        return [make(2, 3 + d, among_zx(d)[2]) for d in range(1, 8)]

    def count_step(stage):
        if stage > 1:
            arrived = count_messages(stage - 1)
            for copy in arrived:
                copy.wait()
            begin = (0, 0, 1, 4)[stage - 1]
            value = counts[stage - 2]
            for n in range(len(arrived)):
                value = value + rcounts[begin + n]
            counts[stage - 1] = value
        if stage < 4:
            for copy in count_messages(stage):
                copy.start()

    def advance(stage, q):
        if stage > 1:
            for copy in arrivals(stage - 1, q):
                copy.wait()
        if stage <= 4:

            @pl.when(q == 0)
            def _():
                count_step(stage)
                if stage == 4:
                    for copy in early[1:3]:
                        copy.wait()
                    for copy in locals_:
                        copy.wait()

        if stage == 2:

            def add1(n, carry):
                yy, zz = n // 4, n % 4
                sums[core, q, yy, zz] = (
                    sums[core, q, yy, zz].astype(F32) + r1[q, yy, zz].astype(F32)
                ).astype(BF)
                return carry

            lax.fori_loop(0, 16, add1, 0)
        elif stage == 3:
            for p in range(4):
                a = sums[core, q, y, p, :, :, 0:LANES].astype(F32)
                b = sums[core, q, p, z, :, :, LANES:PART].astype(F32)
                for d in range(3):
                    a += r2a[q, d, p].astype(F32)
                    b += r2b[q, d, p].astype(F32)
                s2a[q, p] = a.astype(BF)
                s2b[q, p] = b.astype(BF)
        elif stage == 4:
            root = jnp.sqrt(counts[3][0:1, :])
            filters = jnp.where(q < QUARTERS // 2, mine[q % 2], theirs[q % 2])
            a, b = s2a[q, z, x].astype(F32), s2b[q, y, x].astype(F32)
            for d in range(7):
                a += r3a[q, d].astype(F32)
                b += r3b[q, d].astype(F32)
            filtered[core, q, y, z, x, :, 0:LANES] = (
                filters[:, 0:LANES] * (a / root)
            ).astype(BF)
            filtered[core, q, y, z, x, :, LANES:PART] = (
                filters[:, LANES:PART] * (b / root)
            ).astype(BF)
        if stage < STAGES:
            for copy in messages(stage, q):
                copy.start()

    def near(c):
        here = widepos[c + HW].T
        sums_ = [jnp.zeros((CAP, PART), F32) for _ in range(G)]
        for n in range(NB):
            place = c + HW + neigh_ref[c * NB + n]
            shift = jnp.where((cells == 0) & (place < HW), -LENGTH, 0.0) + jnp.where(
                (cells == 63) & (place >= LOCAL + HW), LENGTH, 0.0
            )
            there = widepos[place]
            squared = None
            for p in range(3):
                d = here[:, p : p + 1] - (there[p : p + 1, :] + (shift if p == 0 else 0.0))
                squared = d * d if squared is None else squared + d * d
            block = wide[place]
            for g in range(G):
                weight = jnp.exp(-fall_ref[g] * squared).astype(BF)
                sums_[g] += jnp.dot(weight, block, preferred_element_type=F32)
        rows = pl.ds(pl.multiple_of(c * CAP, CAP), CAP)
        value = merged[rows, :]
        for g in range(G):
            value += sums_[g] * mix_ref[g : g + 1, own_lanes]
        merged[rows, :] = value

    scale_far = 1.0 / math.sqrt(K)

    def far(q, rows):
        value = None
        for n, held in enumerate((cosines, sines)):
            factors = filtered[n, q].reshape(2 * TILE, PART)
            for p in range(2):
                term = jnp.dot(
                    held[2 * q + p, rows, :],
                    factors[p * TILE : (p + 1) * TILE],
                    preferred_element_type=F32,
                )
                value = term if value is None else value + term
        return merged[rows, :] + value * scale_far

    def far_block(q, b):
        rows = pl.ds(pl.multiple_of(b * PIECE, PIECE), PIECE)
        merged[rows, :] = far(q, rows)

    strip = F // TILES

    def fetch(n, held):
        rows = pl.ds(pl.multiple_of(n * strip, strip), strip)
        return copy_of(
            held.at[rows], weights.at[core, rows], wsend_sem, wrecv_sem, n, partner
        )

    def hand_over():
        return copy_of(
            weights.at[core], weights.at[core], wsend_sem, wrecv_sem, TILES, sibling
        )

    def slots(n, carry):
        @pl.when(n == TILES // 2)
        def _():
            early[0].wait()

        @pl.when(n < TILES)
        def _():
            tile(n)

        @pl.when(n == TILES)
        def _():
            for copy in early[3:7]:
                copy.wait()

        @pl.when(n == TILES + 1)
        def _():
            for piece in range(TILES):
                fetch(piece, in_ref).wait()
            hand_over().start()

        @pl.when(n >= TILES)
        def _():
            h = n - TILES
            begin = 3 * h - jnp.maximum(h - 4, 0)
            end = jnp.minimum(begin + 3 - h // 4, LOCAL)
            lax.fori_loop(begin, end, lambda c, carry: (near(c), carry)[1], 0)

        for stage in range(1, STAGES + 1):
            q = (n - stage) // 2

            @pl.when((n >= stage) & ((n - stage) % 2 == 0) & (n < stage + 2 * QUARTERS))
            def _(stage=stage, q=q):
                advance(stage, q)

        for held, side in ((in_ref, 0), (out_ref, 1)):

            @pl.when((n <= TILES) & (core == side))
            def _(held=held):
                fetch(n - 1, held).start()

        @pl.when((n >= STAGES) & ((n - STAGES) % 2 == 0) & (n < STAGES + 2 * QUARTERS - 2))
        def _():
            q = (n - STAGES) // 2
            lax.fori_loop(0, ROWS // PIECE, lambda b, c: (far_block(q, b), c)[1], 0)

        return carry

    tile(0)
    pl.semaphore_wait(barrier, len(peers))
    for copy in early:
        copy.start()
    lax.fori_loop(1, STAGES + 2 * QUARTERS - 1, slots, 0)

    def forth(n):
        return copy_of(outgoing.at[n], incoming.at[n], msend_sem, mrecv_sem, n, partner)

    def home(n):
        return copy_of(back.at[n], returned.at[n], msend_sem, mrecv_sem, PIECES + n, partner)

    def rows_of(side, n):
        return pl.ds(pl.multiple_of(side * HALF + n * PIECE, PIECE), PIECE)

    def give(n, carry):
        rows = rows_of(other, n)
        value = far(QUARTERS - 1, rows)
        merged[rows, :] = value
        outgoing[n] = value.astype(BF)
        forth(n).start()
        return carry

    def keep(n, carry):
        rows = rows_of(waves, n)
        merged[rows, :] = far(QUARTERS - 1, rows)
        return carry

    def mlp(n, carry):
        forth(n).wait()
        rows = rows_of(waves, n)
        own = merged[rows, :]
        their = incoming[n].astype(F32)
        square = jnp.sum(own * own + their * their, axis=1, keepdims=True)
        scale = lax.rsqrt(square * (1.0 / F) + EPS)
        own_n = (own * scale * gain_ref[:, own_lanes]).astype(BF)
        their_n = (their * scale * gain_ref[:, far_lanes]).astype(BF)
        add_own, add_their = own, jnp.zeros_like(own)
        for up, down in ((in_ref, out_ref), (weights.at[0], weights.at[1])):
            hidden = jnp.dot(
                own_n, up[own_lanes, :], preferred_element_type=F32
            ) + jnp.dot(their_n, up[far_lanes, :], preferred_element_type=F32)
            hidden = (hidden / (1.0 + jnp.exp(-hidden))).astype(BF)
            add_own += jnp.dot(hidden, down[:, own_lanes], preferred_element_type=F32)
            add_their += jnp.dot(hidden, down[:, far_lanes], preferred_element_type=F32)
        back[n] = add_their.astype(BF)
        home(n).start()
        result_ref[rows, :] = add_own.astype(BF)
        return carry

    def finish(n, carry):
        home(n).wait()
        rows = rows_of(other, n)
        result_ref[rows, :] = (merged[rows, :] + returned[n].astype(F32)).astype(BF)
        return carry

    lax.fori_loop(0, PIECES, give, 0)
    lax.fori_loop(0, PIECES, keep, 0)
    hand_over().wait()
    lax.fori_loop(0, PIECES, mlp, 0)
    lax.fori_loop(0, PIECES, finish, 0)


def shards(
    features, positions, occupancy, neighbours, wavevectors, filters,
    falloffs, mixing, norm_gain, in_weight, out_weight,
):
    smem = pl.BlockSpec(memory_space=pltpu.SMEM)
    vmem = pl.BlockSpec(memory_space=pltpu.VMEM)
    hbm = pl.BlockSpec(memory_space=pl.ANY)
    half = (QUARTERS, 3, 4, 2, BLOCK, LANES)
    return pl.pallas_call(
        layer,
        in_specs=[smem] * 3 + [vmem] * 7 + [hbm],
        out_specs=vmem,
        out_shape=jax.ShapeDtypeStruct((ROWS, PART), BF),
        scratch_shapes=[
            pltpu.VMEM((LOCAL + 2 * HW, CAP, PART), BF),
            pltpu.VMEM((LOCAL + 2 * HW, 8, CAP), F32),
            pltpu.VMEM((TILES, 8, TILE), F32),
            pltpu.VMEM((ROWS, KP), BF),
            pltpu.VMEM((KP, TILE), BF),
            pltpu.VMEM((TILES, ROWS, TILE), BF),
            pltpu.VMEM((TILES, ROWS, TILE), BF),
            pltpu.VMEM((2, QUARTERS, 4, 4, 2, BLOCK, PART), BF),
            pltpu.VMEM((QUARTERS, 4, 4, 2, BLOCK, PART), BF),
            pltpu.VMEM(half, BF),
            pltpu.VMEM(half, BF),
            pltpu.VMEM((QUARTERS, 4, 2, BLOCK, LANES), BF),
            pltpu.VMEM((QUARTERS, 4, 2, BLOCK, LANES), BF),
            pltpu.VMEM((QUARTERS, 7, BLOCK, LANES), BF),
            pltpu.VMEM((QUARTERS, 7, BLOCK, LANES), BF),
            pltpu.VMEM((2, QUARTERS, 4, 4, 2, BLOCK, PART), BF),
            pltpu.VMEM((2, BLOCK, PART), F32),
            pltpu.VMEM((2, BLOCK, PART), F32),
            pltpu.VMEM((4, 8, LANES), F32),
            pltpu.VMEM((COUNTS, 8, LANES), F32),
            pltpu.VMEM((ROWS, PART), F32),
            pltpu.VMEM((2, *in_weight.shape), BF),
        ]
        + [pltpu.VMEM((PIECES, PIECE, PART), BF)] * 4
        + [pltpu.SemaphoreType.DMA((QUARTERS * MESSAGES,))] * 2
        + [pltpu.SemaphoreType.DMA((COUNTS,))] * 2
        + [pltpu.SemaphoreType.DMA((7,))] * 2
        + [pltpu.SemaphoreType.DMA((2 * PIECES,))] * 2
        + [pltpu.SemaphoreType.DMA((TILES + 1,))] * 2
        + [pltpu.SemaphoreType.DMA((2,))],
        compiler_params=params(collective_id=0, has_side_effects=True),
    )(
        occupancy, neighbours.reshape(LOCAL * NB), falloffs,
        features, positions, wavevectors, mixing, norm_gain[None, :],
        in_weight, out_weight, filters,
    )


def solution(mesh):
    placed = (
        P("cells", "waves"),
        P(None, "cells"),
        P("cells"),
        P("cells", None),
        P(None, "waves"),
        P("waves", None),
        P(),
        P(),
        P(),
        P(None, "waves"),
        P("waves", None),
    )
    return jax.shard_map(
        shards, mesh=mesh, in_specs=placed, out_specs=P("cells", "waves"), check_vma=False
    )
```

```python
import functools
import math

import jax
import jax.numpy as jnp
from jax import lax
from jax.experimental import pallas as pl
from jax.experimental.pallas import tpu as pltpu
from jax.sharding import PartitionSpec as P

F = 512
K = 4096
CAP = 128
HW = 2
NB = 3
G = 4
EPS = 1e-06
WAVES = 2
PART = 256
ROWS = 2048
LOCAL = 16
LENGTH = 1024.0
KP = 64
TILE = 512
TILES = K // TILE
QUARTERS = 4
BLOCK = 32
LANES = 128
HALF = ROWS // 2
BF = jnp.bfloat16
F32 = jnp.float32
MESH = pl.DeviceIdType.MESH
TURN = 1.0 / (2.0 * math.pi)
LOG2E = 1.4426950408889634

SIN = (4.442867900911655, -7.307443330487869, 3.594787161239145, -0.784371485095076)
COS = (1.4142040799995839, -6.977641979004694, 5.715237169770743, -1.7283443233022544)


def params(**more):
    return pltpu.CompilerParams(vmem_limit_bytes=62 << 20, **more)


def split3(v):
    a = v.astype(BF).astype(F32)
    b = (v - a).astype(BF).astype(F32)
    c = ((v - a) - b).astype(BF).astype(F32)
    return a, b, c


def nearest(v):
    return lax.round(v, lax.RoundingMethod.TO_NEAREST_EVEN)


def trig(turns):
    r = turns - nearest(turns)
    s = r * r
    half_sin = r * (SIN[0] + s * (SIN[1] + s * (SIN[2] + s * SIN[3])))
    half_cos = COS[0] + s * (COS[1] + s * (COS[2] + s * COS[3]))
    return (1.0 - half_sin * half_sin).astype(BF), (half_sin * half_cos).astype(BF)


def pieces_of(parts, width):
    row = lax.broadcasted_iota(jnp.int32, (16, width), 0)
    out = jnp.zeros((16, width), F32)
    for n, piece in enumerate(parts):
        out = jnp.where(row == n, jnp.broadcast_to(piece, (16, width)), out)
    return out


def cell_index(z, x, y, core):
    return ((z * 2 + x) * 4 + y) * 2 + core


MESSAGES = 10
COUNTS = 11
STAGES = 7
PIECES = 4
PIECE = HALF // PIECES


def layer(
    occ_ref, neigh_ref, fall_ref,
    feats_ref, pos_ref, wave_ref, mix_ref, gain_ref, in_ref, out_ref, filt_ref,
    result_ref,
    wide, widepos, waves_all, left, right, cosines, sines, sums,
    r1, r2a, r2b, s2a, s2b, r3a, r3b, filtered,
    mine, theirs, counts, rcounts, merged, weights,
    outgoing, incoming, returned,
    send_sem, recv_sem, csend_sem, crecv_sem, esend_sem, erecv_sem, msend_sem, mrecv_sem,
    wsend_sem, wrecv_sem, local_sem,
):
    cells = lax.axis_index("cells")
    waves = lax.axis_index("waves")
    other = 1 - waves
    z, x, y, core = cells // 16, (cells // 8) % 2, (cells // 2) % 4, cells % 2

    def at(cell):
        return {"cells": cell, "waves": waves}

    def along_y(d):
        return at(cell_index(z, x, lax.rem(y + d, 4), core))

    def along_z(d):
        return at(cell_index(lax.rem(z + d, 4), x, y, core))

    def among_zx(d):
        g = lax.rem(z * 2 + x + d, 8)
        return g // 2, g % 2, at(cell_index(g // 2, g % 2, y, core))

    def among_yx(d):
        g = lax.rem(y * 2 + x + d, 8)
        return g // 2, g % 2, at(cell_index(z, g % 2, g // 2, core))

    sibling = at(cell_index(z, x, y, 1 - core))
    above = at(lax.rem(cells + 1, 64))
    below = at(lax.rem(cells + 63, 64))
    partner = {"cells": cells, "waves": other}

    def copy_of(src, dst, sends, receives, n, device):
        return pltpu.make_async_remote_copy(
            src_ref=src, dst_ref=dst, send_sem=sends.at[n], recv_sem=receives.at[n],
            device_id=device, device_id_type=MESH,
        )

    barrier = pltpu.get_barrier_semaphore()
    peers = [sibling, partner, above, below]
    peers += [among(d)[2] for d in range(1, 8) for among in (among_zx, among_yx)]
    for peer in peers:
        pl.semaphore_signal(barrier, inc=1, device_id=peer, device_id_type=MESH)

    for t in range(TILES // 2):
        waves_all[t, 0:3, :] = wave_ref[:, t * TILE : (t + 1) * TILE]
    for c in range(LOCAL):
        widepos[c + HW, 0:3, :] = pos_ref[:, c * CAP : (c + 1) * CAP]
    slot = lax.broadcasted_iota(jnp.int32, (CAP, PART), 0)
    total = jnp.float32(0.0)
    for c in range(LOCAL):
        block = feats_ref[c * CAP : (c + 1) * CAP, :]
        wide[c + HW] = jnp.where(slot < occ_ref[c], block.astype(F32), 0.0).astype(BF)
        total = total + occ_ref[c].astype(F32)
    counts[0] = jnp.full((8, LANES), total)

    index = y * 8 + z * 2 + x
    own_lanes = pl.ds(pl.multiple_of(waves * PART, PART), PART)
    far_lanes = pl.ds(pl.multiple_of(other * PART, PART), PART)

    def filter_rows(half):
        return pl.ds(pl.multiple_of(half * 1024 + index * BLOCK, BLOCK), BLOCK)

    own_tiles, far_tiles = pl.ds(0, TILES // 2), pl.ds(TILES // 2, TILES // 2)
    early = [
        (waves_all.at[own_tiles], waves_all.at[far_tiles], partner),
        (filt_ref.at[filter_rows(0), far_lanes], theirs.at[0], partner),
        (filt_ref.at[filter_rows(1), far_lanes], theirs.at[1], partner),
        (widepos.at[pl.ds(HW, HW)], widepos.at[pl.ds(LOCAL + HW, HW)], below),
        (widepos.at[pl.ds(LOCAL, HW)], widepos.at[pl.ds(0, HW)], above),
        (wide.at[pl.ds(HW, HW)], wide.at[pl.ds(LOCAL + HW, HW)], below),
        (wide.at[pl.ds(LOCAL, HW)], wide.at[pl.ds(0, HW)], above),
    ]
    early = [
        copy_of(src, dst, esend_sem, erecv_sem, n, device)
        for n, (src, dst, device) in enumerate(early)
    ]
    locals_ = [
        pltpu.make_async_copy(
            filt_ref.at[filter_rows(h), own_lanes], mine.at[h], local_sem.at[h]
        )
        for h in range(2)
    ]
    for copy in locals_:
        copy.start()

    first = cells * LOCAL
    cell_of = lax.broadcasted_iota(jnp.int32, (1, ROWS), 1) // CAP
    parts = []
    for p in range(3):
        v = pos_ref[p : p + 1, :]
        if p == 0:
            v = v - (cell_of + first).astype(F32)
        a, b, _ = split3(v)
        parts += [a, a, b, b]
    row = lax.broadcasted_iota(jnp.int32, (16, ROWS), 0)
    hot = (row == lax.broadcasted_iota(jnp.int32, (16, ROWS), 1) // CAP).astype(F32)
    left[...] = jnp.concatenate([pieces_of(parts, ROWS), hot, hot, hot], axis=0).T.astype(BF)
    merged[...] = feats_ref[...].astype(F32)

    def tile(i):
        waves_here = waves_all[i]
        parts = []
        for p in range(3):
            k1, k2, _ = split3(waves_here[p : p + 1, :] * TURN)
            parts += [k1, k2, k1, k2]
        cell = (lax.broadcasted_iota(jnp.int32, (16, TILE), 0) + first).astype(F32)
        whole = cell * (waves_here[0:1, :] * TURN)
        whole = whole - nearest(whole)
        right[...] = jnp.concatenate([pieces_of(parts, TILE), *split3(whole)], axis=0).astype(BF)
        for b in range(ROWS // 512):
            rows = slice(b * 512, (b + 1) * 512)
            turns = jnp.dot(left[rows, :], right[...], preferred_element_type=F32)
            cosine, sine = trig(turns)
            cosines[i, rows, :] = cosine
            sines[i, rows, :] = sine
        atoms = wide[HW : HW + LOCAL].reshape(ROWS, PART)
        q, p = i // 2, i % 2
        for n, held in enumerate((cosines, sines)):
            part = lax.dot_general(
                held[i], atoms, (((0,), (0,)), ((), ())), preferred_element_type=F32
            )
            sums[n, q, pl.ds(2 * p, 2)] = part.astype(BF).reshape(2, 4, 2, BLOCK, PART)

    lane_a, lane_b = pl.ds(0, LANES), pl.ds(LANES, LANES)

    def messages(stage, q):
        base = q * MESSAGES
        out = []

        def add(src, dst, n, device):
            out.append(copy_of(src, dst, send_sem, recv_sem, base + n, device))

        if stage == 1:
            add(sums.at[1 - core, q], r1.at[q], 0, sibling)
        elif stage == 6:
            piece = filtered.at[core, q]
            add(piece, piece, 1, sibling)
        elif stage in (2, 5):
            for d in (1, 2, 3):
                ty, tz, m = lax.rem(y + d, 4), lax.rem(z + d, 4), d - 1
                if stage == 2:
                    add(sums.at[core, q, ty, :, :, :, lane_a], r2a.at[q, m], 2, along_y(d))
                    add(sums.at[core, q, :, tz, :, :, lane_b], r2b.at[q, m], 3, along_z(d))
                else:
                    piece = filtered.at[core, q, y, :, :, :, lane_a]
                    add(piece, piece, 4, along_y(d))
                    piece = filtered.at[core, q, :, z, :, :, lane_b]
                    add(piece, piece, 5, along_z(d))
        else:
            for d in range(1, 8):
                m = d - 1
                if stage == 3:
                    tz, tx, device = among_zx(d)
                    add(s2a.at[q, tz, tx], r3a.at[q, m], 6, device)
                    ty, tx, device = among_yx(d)
                    add(s2b.at[q, ty, tx], r3b.at[q, m], 7, device)
                else:
                    piece = filtered.at[core, q, y, z, x, :, lane_a]
                    add(piece, piece, 8, among_zx(d)[2])
                    piece = filtered.at[core, q, y, z, x, :, lane_b]
                    add(piece, piece, 9, among_yx(d)[2])
        return out

    def arrivals(stage, q):
        if stage in (1, 6):
            return messages(stage, q)
        first, a, b = {2: (2, r2a, r2b), 3: (6, r3a, r3b), 4: (8, r3a, r3b), 5: (4, r2a, r2b)}[stage]
        return [
            copy_of(
                held.at[q], held.at[q], send_sem, recv_sem,
                q * MESSAGES + first + n, sibling,
            )
            for n, held in enumerate((a, b))
        ]

    def count_messages(stage):
        def make(src, n, device):
            return copy_of(counts.at[src], rcounts.at[n], csend_sem, crecv_sem, n, device)

        if stage == 1:
            return [make(0, 0, sibling)]
        if stage == 2:
            return [make(1, d, along_y(d)) for d in (1, 2, 3)]
        return [make(2, 3 + d, among_zx(d)[2]) for d in range(1, 8)]

    def count_step(stage):
        if stage > 1:
            arrived = count_messages(stage - 1)
            for copy in arrived:
                copy.wait()
            begin = (0, 0, 1, 4)[stage - 1]
            value = counts[stage - 2]
            for n in range(len(arrived)):
                value = value + rcounts[begin + n]
            counts[stage - 1] = value
        if stage < 4:
            for copy in count_messages(stage):
                copy.start()

    def advance(stage, q):
        if stage > 1:
            for copy in arrivals(stage - 1, q):
                copy.wait()
        if stage <= 4:

            @pl.when(q == 0)
            def _():
                count_step(stage)
                if stage == 4:
                    for copy in early[1:3]:
                        copy.wait()
                    for copy in locals_:
                        copy.wait()

        if stage == 2:

            def add1(n, carry):
                yy, zz = n // 4, n % 4
                sums[core, q, yy, zz] = (
                    sums[core, q, yy, zz].astype(F32) + r1[q, yy, zz].astype(F32)
                ).astype(BF)
                return carry

            lax.fori_loop(0, 16, add1, 0)
        elif stage == 3:
            for p in range(4):
                a = sums[core, q, y, p, :, :, 0:LANES].astype(F32)
                b = sums[core, q, p, z, :, :, LANES:PART].astype(F32)
                for d in range(3):
                    a += r2a[q, d, p].astype(F32)
                    b += r2b[q, d, p].astype(F32)
                s2a[q, p] = a.astype(BF)
                s2b[q, p] = b.astype(BF)
        elif stage == 4:
            root = jnp.sqrt(counts[3][0:1, :])
            filters = jnp.where(q < QUARTERS // 2, mine[q % 2], theirs[q % 2])
            a, b = s2a[q, z, x].astype(F32), s2b[q, y, x].astype(F32)
            for d in range(7):
                a += r3a[q, d].astype(F32)
                b += r3b[q, d].astype(F32)
            filtered[core, q, y, z, x, :, 0:LANES] = (
                filters[:, 0:LANES] * (a / root)
            ).astype(BF)
            filtered[core, q, y, z, x, :, LANES:PART] = (
                filters[:, LANES:PART] * (b / root)
            ).astype(BF)
        if stage < STAGES:
            for copy in messages(stage, q):
                copy.start()

    def near(c):
        here = widepos[c + HW].T
        sums_ = [jnp.zeros((CAP, PART), F32) for _ in range(G)]
        for n in range(NB):
            place = c + HW + neigh_ref[c * NB + n]
            shift = jnp.where((cells == 0) & (place < HW), -LENGTH, 0.0) + jnp.where(
                (cells == 63) & (place >= LOCAL + HW), LENGTH, 0.0
            )
            there = widepos[place]
            squared = None
            for p in range(3):
                d = here[:, p : p + 1] - (there[p : p + 1, :] + (shift if p == 0 else 0.0))
                squared = d * d if squared is None else squared + d * d
            block = wide[place]
            for g in range(G):
                weight = jnp.exp(-fall_ref[g] * squared).astype(BF)
                sums_[g] += jnp.dot(weight, block, preferred_element_type=F32)
        rows = pl.ds(pl.multiple_of(c * CAP, CAP), CAP)
        value = merged[rows, :]
        for g in range(G):
            value += sums_[g] * mix_ref[g : g + 1, own_lanes]
        merged[rows, :] = value

    scale_far = 1.0 / math.sqrt(K)

    def far(q, rows):
        value = None
        for n, held in enumerate((cosines, sines)):
            factors = filtered[n, q].reshape(2 * TILE, PART)
            for p in range(2):
                term = jnp.dot(
                    held[2 * q + p, rows, :],
                    factors[p * TILE : (p + 1) * TILE],
                    preferred_element_type=F32,
                )
                value = term if value is None else value + term
        return merged[rows, :] + value * scale_far

    def far_block(q, b):
        rows = pl.ds(pl.multiple_of(b * PIECE, PIECE), PIECE)
        merged[rows, :] = far(q, rows)

    strip = F // TILES

    def fetch(n, held):
        rows = pl.ds(pl.multiple_of(n * strip, strip), strip)
        return copy_of(
            held.at[rows], weights.at[core, rows], wsend_sem, wrecv_sem, n, partner
        )

    def hand_over():
        return copy_of(
            weights.at[core], weights.at[core], wsend_sem, wrecv_sem, TILES, sibling
        )

    reached = (
        (1, 3, 5, 7), (2, 4, 6, 8), (4, 6, 8, 9), (6, 8, 9, 10),
        (8, 9, 10, 11), (9, 10, 11, 12), (10, 11, 12, 13),
    )

    def chunk_at(n, choices):
        q = jnp.int32(0)
        for choice in choices[:-1]:
            q = q + jnp.where(n > choice, 1, 0)
        return q

    def any_of(value, choices):
        found = value == choices[0]
        for choice in choices[1:]:
            found = found | (value == choice)
        return found

    def slots(n, carry):
        @pl.when(n == TILES // 2)
        def _():
            early[0].wait()

        @pl.when(n < TILES)
        def _():
            tile(n)

        @pl.when(n == 0)
        def _():
            pl.semaphore_wait(barrier, len(peers))
            for copy in early:
                copy.start()

        @pl.when(n == TILES)
        def _():
            for copy in early[3:7]:
                copy.wait()

        @pl.when(n == TILES + 1)
        def _():
            for piece in range(TILES):
                fetch(piece, in_ref).wait()
            hand_over().start()

        @pl.when(n >= TILES)
        def _():
            h = n - TILES
            begin = 3 * h - jnp.maximum(h - 4, 0)
            end = jnp.minimum(begin + 3 - h // 4, LOCAL)
            lax.fori_loop(begin, end, lambda c, carry: (near(c), carry)[1], 0)

        for stage in range(1, STAGES + 1):
            slots_of = reached[stage - 1]

            @pl.when(any_of(n, slots_of))
            def _(stage=stage, q=chunk_at(n, slots_of)):
                advance(stage, q)

        for held, side in ((in_ref, 0), (out_ref, 1)):

            @pl.when((n >= 1) & (n <= TILES) & (core == side))
            def _(held=held):
                fetch(n - 1, held).start()

        @pl.when(any_of(n, reached[-1][:-1]))
        def _():
            q = chunk_at(n, reached[-1])
            lax.fori_loop(0, ROWS // PIECE, lambda b, c: (far_block(q, b), c)[1], 0)

        return carry

    lax.fori_loop(0, STAGES + 2 * QUARTERS - 1, slots, 0)

    def forth(n):
        return copy_of(outgoing.at[n], incoming.at[n], msend_sem, mrecv_sem, n, partner)

    def home(n):
        return copy_of(outgoing.at[n], returned.at[n], msend_sem, mrecv_sem, PIECES + n, partner)

    def rows_of(side, n):
        return pl.ds(pl.multiple_of(side * HALF + n * PIECE, PIECE), PIECE)

    def give(n, carry):
        rows = rows_of(other, n)
        value = far(QUARTERS - 1, rows)
        merged[rows, :] = value
        outgoing[n] = value.astype(BF)
        forth(n).start()
        return carry

    def keep(n, carry):
        rows = rows_of(waves, n)
        merged[rows, :] = far(QUARTERS - 1, rows)
        return carry

    def mlp(n, carry):
        forth(n).wait()
        rows = rows_of(waves, n)
        own = merged[rows, :]
        their = incoming[n].astype(F32)
        square = jnp.sum(own * own + their * their, axis=1, keepdims=True)
        scale = lax.rsqrt(square * (1.0 / F) + EPS)
        own_n = (own * scale * gain_ref[:, own_lanes]).astype(BF)
        their_n = (their * scale * gain_ref[:, far_lanes]).astype(BF)
        add_own, add_their = own, jnp.zeros_like(own)
        for up, down in ((in_ref, out_ref), (weights.at[0], weights.at[1])):
            hidden = jnp.dot(
                own_n, up[own_lanes, :], preferred_element_type=F32
            ) + jnp.dot(their_n, up[far_lanes, :], preferred_element_type=F32)
            hidden = (hidden / (1.0 + jnp.exp(-hidden))).astype(BF)
            add_own += jnp.dot(hidden, down[:, own_lanes], preferred_element_type=F32)
            add_their += jnp.dot(hidden, down[:, far_lanes], preferred_element_type=F32)
        outgoing[n] = add_their.astype(BF)
        home(n).start()
        result_ref[rows, :] = add_own.astype(BF)
        return carry

    def finish(n, carry):
        home(n).wait()
        rows = rows_of(other, n)
        result_ref[rows, :] = (merged[rows, :] + returned[n].astype(F32)).astype(BF)
        return carry

    lax.fori_loop(0, PIECES, give, 0)
    lax.fori_loop(0, PIECES, keep, 0)
    hand_over().wait()
    lax.fori_loop(0, PIECES, mlp, 0)
    lax.fori_loop(0, PIECES, finish, 0)


def shards(
    features, positions, occupancy, neighbours, wavevectors, filters,
    falloffs, mixing, norm_gain, in_weight, out_weight,
):
    smem = pl.BlockSpec(memory_space=pltpu.SMEM)
    vmem = pl.BlockSpec(memory_space=pltpu.VMEM)
    hbm = pl.BlockSpec(memory_space=pl.ANY)
    half = (QUARTERS, 3, 4, 2, BLOCK, LANES)
    return pl.pallas_call(
        layer,
        in_specs=[smem] * 3 + [vmem] * 7 + [hbm],
        out_specs=vmem,
        out_shape=jax.ShapeDtypeStruct((ROWS, PART), BF),
        scratch_shapes=[
            pltpu.VMEM((LOCAL + 2 * HW, CAP, PART), BF),
            pltpu.VMEM((LOCAL + 2 * HW, 8, CAP), F32),
            pltpu.VMEM((TILES, 8, TILE), F32),
            pltpu.VMEM((ROWS, KP), BF),
            pltpu.VMEM((KP, TILE), BF),
            pltpu.VMEM((TILES, ROWS, TILE), BF),
            pltpu.VMEM((TILES, ROWS, TILE), BF),
            pltpu.VMEM((2, QUARTERS, 4, 4, 2, BLOCK, PART), BF),
            pltpu.VMEM((QUARTERS, 4, 4, 2, BLOCK, PART), BF),
            pltpu.VMEM(half, BF),
            pltpu.VMEM(half, BF),
            pltpu.VMEM((QUARTERS, 4, 2, BLOCK, LANES), BF),
            pltpu.VMEM((QUARTERS, 4, 2, BLOCK, LANES), BF),
            pltpu.VMEM((QUARTERS, 7, BLOCK, LANES), BF),
            pltpu.VMEM((QUARTERS, 7, BLOCK, LANES), BF),
            pltpu.VMEM((2, QUARTERS, 4, 4, 2, BLOCK, PART), BF),
            pltpu.VMEM((2, BLOCK, PART), F32),
            pltpu.VMEM((2, BLOCK, PART), F32),
            pltpu.VMEM((4, 8, LANES), F32),
            pltpu.VMEM((COUNTS, 8, LANES), F32),
            pltpu.VMEM((ROWS, PART), F32),
            pltpu.VMEM((2, *in_weight.shape), BF),
        ]
        + [pltpu.VMEM((PIECES, PIECE, PART), BF)] * 3
        + [pltpu.SemaphoreType.DMA((QUARTERS * MESSAGES,))] * 2
        + [pltpu.SemaphoreType.DMA((COUNTS,))] * 2
        + [pltpu.SemaphoreType.DMA((7,))] * 2
        + [pltpu.SemaphoreType.DMA((2 * PIECES,))] * 2
        + [pltpu.SemaphoreType.DMA((TILES + 1,))] * 2
        + [pltpu.SemaphoreType.DMA((2,))],
        compiler_params=params(collective_id=0, has_side_effects=True),
    )(
        occupancy, neighbours.reshape(LOCAL * NB), falloffs,
        features, positions, wavevectors, mixing, norm_gain[None, :],
        in_weight, out_weight, filters,
    )


def solution(mesh):
    placed = (
        P("cells", "waves"),
        P(None, "cells"),
        P("cells"),
        P("cells", None),
        P(None, "waves"),
        P("waves", None),
        P(),
        P(),
        P(),
        P(None, "waves"),
        P("waves", None),
    )
    return jax.shard_map(
        shards, mesh=mesh, in_specs=placed, out_specs=P("cells", "waves"), check_vma=False
    )
```

```python
import functools
import math

import jax
import jax.numpy as jnp
from jax import lax
from jax.experimental import pallas as pl
from jax.experimental.pallas import tpu as pltpu
from jax.sharding import PartitionSpec as P

F = 512
K = 4096
CAP = 128
HW = 2
NB = 3
G = 4
EPS = 1e-06
WAVES = 2
PART = 256
ROWS = 2048
LOCAL = 16
LENGTH = 1024.0
KP = 64
TILE = 512
TILES = K // TILE
QUARTERS = 4
BLOCK = 32
LANES = 128
HALF = ROWS // 2
BF = jnp.bfloat16
F32 = jnp.float32
MESH = pl.DeviceIdType.MESH
TURN = 1.0 / (2.0 * math.pi)
LOG2E = 1.4426950408889634

SIN = (4.442867900911655, -7.307443330487869, 3.594787161239145, -0.784371485095076)
COS = (1.4142040799995839, -6.977641979004694, 5.715237169770743, -1.7283443233022544)


def params(**more):
    return pltpu.CompilerParams(vmem_limit_bytes=65400 << 10, **more)


def split3(v):
    a = v.astype(BF).astype(F32)
    b = (v - a).astype(BF).astype(F32)
    c = ((v - a) - b).astype(BF).astype(F32)
    return a, b, c


def nearest(v):
    return lax.round(v, lax.RoundingMethod.TO_NEAREST_EVEN)


def trig(turns):
    r = turns - nearest(turns)
    s = r * r
    half_sin = r * (SIN[0] + s * (SIN[1] + s * (SIN[2] + s * SIN[3])))
    half_cos = COS[0] + s * (COS[1] + s * (COS[2] + s * COS[3]))
    return (1.0 - half_sin * half_sin).astype(BF), (half_sin * half_cos).astype(BF)


def pieces_of(parts, width):
    row = lax.broadcasted_iota(jnp.int32, (16, width), 0)
    out = jnp.zeros((16, width), F32)
    for n, piece in enumerate(parts):
        out = jnp.where(row == n, jnp.broadcast_to(piece, (16, width)), out)
    return out


def cell_index(z, x, y, core):
    return ((z * 2 + x) * 4 + y) * 2 + core


MESSAGES = 10
COUNTS = 11
STAGES = 7
PIECES = 4
PIECE = HALF // PIECES


def layer(
    occ_ref, neigh_ref, fall_ref,
    feats_ref, pos_ref, wave_ref, mix_ref, gain_ref, in_ref, out_ref, filt_ref,
    result_ref,
    wide, widepos, waves_all, left, right, cosines, sines, sums,
    r1, r2a, r2b, s2a, s2b, r3a, r3b, filtered,
    mine, theirs, counts, rcounts, merged, weights,
    outgoing, incoming, returned,
    send_sem, recv_sem, csend_sem, crecv_sem, esend_sem, erecv_sem, msend_sem, mrecv_sem,
    wsend_sem, wrecv_sem, local_sem,
):
    cells = lax.axis_index("cells")
    waves = lax.axis_index("waves")
    other = 1 - waves
    z, x, y, core = cells // 16, (cells // 8) % 2, (cells // 2) % 4, cells % 2

    def at(cell):
        return {"cells": cell, "waves": waves}

    def along_y(d):
        return at(cell_index(z, x, lax.rem(y + d, 4), core))

    def along_z(d):
        return at(cell_index(lax.rem(z + d, 4), x, y, core))

    def among_zx(d):
        g = lax.rem(z * 2 + x + d, 8)
        return g // 2, g % 2, at(cell_index(g // 2, g % 2, y, core))

    def among_yx(d):
        g = lax.rem(y * 2 + x + d, 8)
        return g // 2, g % 2, at(cell_index(z, g % 2, g // 2, core))

    sibling = at(cell_index(z, x, y, 1 - core))
    above = at(lax.rem(cells + 1, 64))
    below = at(lax.rem(cells + 63, 64))
    partner = {"cells": cells, "waves": other}

    def copy_of(src, dst, sends, receives, n, device):
        return pltpu.make_async_remote_copy(
            src_ref=src, dst_ref=dst, send_sem=sends.at[n], recv_sem=receives.at[n],
            device_id=device, device_id_type=MESH,
        )

    barrier = pltpu.get_barrier_semaphore()
    peers = [sibling, partner, above, below]
    peers += [among(d)[2] for d in range(1, 8) for among in (among_zx, among_yx)]
    for peer in peers:
        pl.semaphore_signal(barrier, inc=1, device_id=peer, device_id_type=MESH)

    for t in range(TILES // 2):
        waves_all[t, 0:3, :] = wave_ref[:, t * TILE : (t + 1) * TILE]
    for c in range(LOCAL):
        widepos[c + HW, 0:3, :] = pos_ref[:, c * CAP : (c + 1) * CAP]
    slot = lax.broadcasted_iota(jnp.int32, (CAP, PART), 0)
    total = jnp.float32(0.0)
    for c in range(LOCAL):
        block = feats_ref[c * CAP : (c + 1) * CAP, :]
        wide[c + HW] = jnp.where(slot < occ_ref[c], block.astype(F32), 0.0).astype(BF)
        total = total + occ_ref[c].astype(F32)
    counts[0] = jnp.full((8, LANES), total)

    index = y * 8 + z * 2 + x
    own_lanes = pl.ds(pl.multiple_of(waves * PART, PART), PART)
    far_lanes = pl.ds(pl.multiple_of(other * PART, PART), PART)

    def filter_rows(half):
        return pl.ds(pl.multiple_of(half * 1024 + index * BLOCK, BLOCK), BLOCK)

    own_tiles, far_tiles = pl.ds(0, TILES // 2), pl.ds(TILES // 2, TILES // 2)
    early = [
        (waves_all.at[own_tiles], waves_all.at[far_tiles], partner),
        (filt_ref.at[filter_rows(0), far_lanes], theirs.at[0], partner),
        (filt_ref.at[filter_rows(1), far_lanes], theirs.at[1], partner),
        (widepos.at[pl.ds(HW, HW)], widepos.at[pl.ds(LOCAL + HW, HW)], below),
        (widepos.at[pl.ds(LOCAL, HW)], widepos.at[pl.ds(0, HW)], above),
        (wide.at[pl.ds(HW, HW)], wide.at[pl.ds(LOCAL + HW, HW)], below),
        (wide.at[pl.ds(LOCAL, HW)], wide.at[pl.ds(0, HW)], above),
    ]
    early = [
        copy_of(src, dst, esend_sem, erecv_sem, n, device)
        for n, (src, dst, device) in enumerate(early)
    ]
    locals_ = [
        pltpu.make_async_copy(
            filt_ref.at[filter_rows(h), own_lanes], mine.at[h], local_sem.at[h]
        )
        for h in range(2)
    ]
    for copy in locals_:
        copy.start()

    first = cells * LOCAL
    cell_of = lax.broadcasted_iota(jnp.int32, (1, ROWS), 1) // CAP
    parts = []
    for p in range(3):
        v = pos_ref[p : p + 1, :]
        if p == 0:
            v = v - (cell_of + first).astype(F32)
        a, b, _ = split3(v)
        parts += [a, a, b, b]
    row = lax.broadcasted_iota(jnp.int32, (16, ROWS), 0)
    hot = (row == lax.broadcasted_iota(jnp.int32, (16, ROWS), 1) // CAP).astype(F32)
    left[...] = jnp.concatenate([pieces_of(parts, ROWS), hot, hot, hot], axis=0).T.astype(BF)
    merged[...] = feats_ref[...].astype(F32)

    def tile(i):
        waves_here = waves_all[i]
        parts = []
        for p in range(3):
            k1, k2, _ = split3(waves_here[p : p + 1, :] * TURN)
            parts += [k1, k2, k1, k2]
        cell = (lax.broadcasted_iota(jnp.int32, (16, TILE), 0) + first).astype(F32)
        whole = cell * (waves_here[0:1, :] * TURN)
        whole = whole - nearest(whole)
        right[...] = jnp.concatenate([pieces_of(parts, TILE), *split3(whole)], axis=0).astype(BF)
        totals = [None, None]
        values = None
        for b in range(ROWS // HALF + 1):
            if b > 0:
                atoms = wide[HW + (b - 1) * 8 : HW + b * 8].reshape(HALF, PART)
                for n, value in enumerate(values):
                    part = lax.dot_general(
                        value, atoms, (((0,), (0,)), ((), ())), preferred_element_type=F32
                    )
                    totals[n] = part if totals[n] is None else totals[n] + part
            if b < ROWS // HALF:
                rows = slice(b * HALF, (b + 1) * HALF)
                turns = jnp.dot(left[rows, :], right[...], preferred_element_type=F32)
                values = trig(turns)
                cosines[i, rows, :], sines[i, rows, :] = values
        q, p = i // 2, i % 2
        for n, part in enumerate(totals):
            sums[n, q, pl.ds(2 * p, 2)] = part.astype(BF).reshape(2, 4, 2, BLOCK, PART)

    lane_a, lane_b = pl.ds(0, LANES), pl.ds(LANES, LANES)

    def messages(stage, q):
        base = q * MESSAGES
        out = []

        def add(src, dst, n, device):
            out.append(copy_of(src, dst, send_sem, recv_sem, base + n, device))

        if stage == 1:
            add(sums.at[1 - core, q], r1.at[q], 0, sibling)
        elif stage == 6:
            piece = filtered.at[core, q]
            add(piece, piece, 1, sibling)
        elif stage in (2, 5):
            for d in (1, 2, 3):
                ty, tz, m = lax.rem(y + d, 4), lax.rem(z + d, 4), d - 1
                if stage == 2:
                    add(sums.at[core, q, ty, :, :, :, lane_a], r2a.at[q, m], 2, along_y(d))
                    add(sums.at[core, q, :, tz, :, :, lane_b], r2b.at[q, m], 3, along_z(d))
                else:
                    piece = filtered.at[core, q, y, :, :, :, lane_a]
                    add(piece, piece, 4, along_y(d))
                    piece = filtered.at[core, q, :, z, :, :, lane_b]
                    add(piece, piece, 5, along_z(d))
        else:
            for d in range(1, 8):
                m = d - 1
                if stage == 3:
                    tz, tx, device = among_zx(d)
                    add(s2a.at[q, tz, tx], r3a.at[q, m], 6, device)
                    ty, tx, device = among_yx(d)
                    add(s2b.at[q, ty, tx], r3b.at[q, m], 7, device)
                else:
                    piece = filtered.at[core, q, y, z, x, :, lane_a]
                    add(piece, piece, 8, among_zx(d)[2])
                    piece = filtered.at[core, q, y, z, x, :, lane_b]
                    add(piece, piece, 9, among_yx(d)[2])
        return out

    def arrivals(stage, q):
        if stage in (1, 6):
            return messages(stage, q)
        first, a, b = {2: (2, r2a, r2b), 3: (6, r3a, r3b), 4: (8, r3a, r3b), 5: (4, r2a, r2b)}[stage]
        return [
            copy_of(
                held.at[q], held.at[q], send_sem, recv_sem,
                q * MESSAGES + first + n, sibling,
            )
            for n, held in enumerate((a, b))
        ]

    def count_messages(stage):
        def make(src, n, device):
            return copy_of(counts.at[src], rcounts.at[n], csend_sem, crecv_sem, n, device)

        if stage == 1:
            return [make(0, 0, sibling)]
        if stage == 2:
            return [make(1, d, along_y(d)) for d in (1, 2, 3)]
        return [make(2, 3 + d, among_zx(d)[2]) for d in range(1, 8)]

    def count_step(stage):
        if stage > 1:
            arrived = count_messages(stage - 1)
            for copy in arrived:
                copy.wait()
            begin = (0, 0, 1, 4)[stage - 1]
            value = counts[stage - 2]
            for n in range(len(arrived)):
                value = value + rcounts[begin + n]
            counts[stage - 1] = value
        if stage < 4:
            for copy in count_messages(stage):
                copy.start()

    def advance(stage, q):
        if stage > 1:
            for copy in arrivals(stage - 1, q):
                copy.wait()
        if stage <= 4:

            @pl.when(q == 0)
            def _():
                count_step(stage)
                if stage == 4:
                    for copy in early[1:3]:
                        copy.wait()
                    for copy in locals_:
                        copy.wait()

        if stage == 2:

            def add1(n, carry):
                yy, zz = n // 4, n % 4
                sums[core, q, yy, zz] = (
                    sums[core, q, yy, zz].astype(F32) + r1[q, yy, zz].astype(F32)
                ).astype(BF)
                return carry

            lax.fori_loop(0, 16, add1, 0)
        elif stage == 3:
            for p in range(4):
                a = sums[core, q, y, p, :, :, 0:LANES].astype(F32)
                b = sums[core, q, p, z, :, :, LANES:PART].astype(F32)
                for d in range(3):
                    a += r2a[q, d, p].astype(F32)
                    b += r2b[q, d, p].astype(F32)
                s2a[q, p] = a.astype(BF)
                s2b[q, p] = b.astype(BF)
        elif stage == 4:
            root = jnp.sqrt(counts[3][0:1, :])
            filters = jnp.where(q < QUARTERS // 2, mine[q % 2], theirs[q % 2])
            a, b = s2a[q, z, x].astype(F32), s2b[q, y, x].astype(F32)
            for d in range(7):
                a += r3a[q, d].astype(F32)
                b += r3b[q, d].astype(F32)
            filtered[core, q, y, z, x, :, 0:LANES] = (
                filters[:, 0:LANES] * (a / root)
            ).astype(BF)
            filtered[core, q, y, z, x, :, LANES:PART] = (
                filters[:, LANES:PART] * (b / root)
            ).astype(BF)
        if stage < STAGES:
            for copy in messages(stage, q):
                copy.start()

    def near(c):
        here = widepos[c + HW].T
        sums_ = [jnp.zeros((CAP, PART), F32) for _ in range(G)]
        for n in range(NB):
            place = c + HW + neigh_ref[c * NB + n]
            shift = jnp.where((cells == 0) & (place < HW), -LENGTH, 0.0) + jnp.where(
                (cells == 63) & (place >= LOCAL + HW), LENGTH, 0.0
            )
            there = widepos[place]
            squared = None
            for p in range(3):
                d = here[:, p : p + 1] - (there[p : p + 1, :] + (shift if p == 0 else 0.0))
                squared = d * d if squared is None else squared + d * d
            block = wide[place]
            for g in range(G):
                weight = jnp.exp(-fall_ref[g] * squared).astype(BF)
                sums_[g] += jnp.dot(weight, block, preferred_element_type=F32)
        rows = pl.ds(pl.multiple_of(c * CAP, CAP), CAP)
        value = merged[rows, :]
        for g in range(G):
            value += sums_[g] * mix_ref[g : g + 1, own_lanes]
        merged[rows, :] = value

    scale_far = 1.0 / math.sqrt(K)

    def far(q, rows):
        value = None
        for n, held in enumerate((cosines, sines)):
            factors = filtered[n, q].reshape(2 * TILE, PART)
            for p in range(2):
                term = jnp.dot(
                    held[2 * q + p, rows, :],
                    factors[p * TILE : (p + 1) * TILE],
                    preferred_element_type=F32,
                )
                value = term if value is None else value + term
        return merged[rows, :] + value * scale_far

    def far_block(q, b):
        rows = pl.ds(pl.multiple_of(b * PIECE, PIECE), PIECE)
        merged[rows, :] = far(q, rows)

    strip = F // TILES

    def fetch(n, held):
        rows = pl.ds(pl.multiple_of(n * strip, strip), strip)
        return copy_of(
            held.at[rows], weights.at[core, rows], wsend_sem, wrecv_sem, n, partner
        )

    def hand_over():
        return copy_of(
            weights.at[core], weights.at[core], wsend_sem, wrecv_sem, TILES, sibling
        )

    reached = (
        (1, 3, 5, 7), (2, 4, 6, 8), (4, 6, 8, 9), (6, 8, 9, 10),
        (8, 9, 10, 11), (9, 10, 11, 12), (10, 11, 12, 13),
    )

    def chunk_at(n, choices):
        q = jnp.int32(0)
        for choice in choices[:-1]:
            q = q + jnp.where(n > choice, 1, 0)
        return q

    def any_of(value, choices):
        found = value == choices[0]
        for choice in choices[1:]:
            found = found | (value == choice)
        return found

    def slots(n, carry):
        @pl.when(n == TILES // 2)
        def _():
            early[0].wait()

        @pl.when(n < TILES)
        def _():
            tile(n)

        @pl.when(n == 0)
        def _():
            pl.semaphore_wait(barrier, len(peers))
            for copy in early:
                copy.start()

        @pl.when(n == TILES)
        def _():
            for copy in early[3:7]:
                copy.wait()

        @pl.when(n == TILES + 1)
        def _():
            for piece in range(TILES):
                fetch(piece, in_ref).wait()
            hand_over().start()

        @pl.when(n >= TILES)
        def _():
            h = n - TILES
            begin = 3 * h - jnp.maximum(h - 4, 0)
            end = jnp.minimum(begin + 3 - h // 4, LOCAL)
            lax.fori_loop(begin, end, lambda c, carry: (near(c), carry)[1], 0)

        for stage in range(1, STAGES + 1):
            slots_of = reached[stage - 1]

            @pl.when(any_of(n, slots_of))
            def _(stage=stage, q=chunk_at(n, slots_of)):
                advance(stage, q)

        for held, side in ((in_ref, 0), (out_ref, 1)):

            @pl.when((n >= 1) & (n <= TILES) & (core == side))
            def _(held=held):
                fetch(n - 1, held).start()

        @pl.when(any_of(n, reached[-1][:-1]))
        def _():
            q = chunk_at(n, reached[-1])
            lax.fori_loop(0, ROWS // PIECE, lambda b, c: (far_block(q, b), c)[1], 0)

        return carry

    lax.fori_loop(0, STAGES + 2 * QUARTERS - 1, slots, 0)

    def forth(n):
        return copy_of(outgoing.at[n], incoming.at[n], msend_sem, mrecv_sem, n, partner)

    def home(n):
        return copy_of(outgoing.at[n], returned.at[n], msend_sem, mrecv_sem, PIECES + n, partner)

    def rows_of(side, n):
        return pl.ds(pl.multiple_of(side * HALF + n * PIECE, PIECE), PIECE)

    def give(n, carry):
        rows = rows_of(other, n)
        value = far(QUARTERS - 1, rows)
        merged[rows, :] = value
        outgoing[n] = value.astype(BF)
        forth(n).start()
        return carry

    def keep(n, carry):
        rows = rows_of(waves, n)
        merged[rows, :] = far(QUARTERS - 1, rows)
        return carry

    def mlp(n, carry):
        forth(n).wait()
        rows = rows_of(waves, n)
        own = merged[rows, :]
        their = incoming[n].astype(F32)
        square = jnp.sum(own * own + their * their, axis=1, keepdims=True)
        scale = lax.rsqrt(square * (1.0 / F) + EPS)
        own_n = (own * scale * gain_ref[:, own_lanes]).astype(BF)
        their_n = (their * scale * gain_ref[:, far_lanes]).astype(BF)
        add_own, add_their = own, jnp.zeros_like(own)
        for up, down in ((in_ref, out_ref), (weights.at[0], weights.at[1])):
            hidden = jnp.dot(
                own_n, up[own_lanes, :], preferred_element_type=F32
            ) + jnp.dot(their_n, up[far_lanes, :], preferred_element_type=F32)
            hidden = (hidden / (1.0 + jnp.exp(-hidden))).astype(BF)
            add_own += jnp.dot(hidden, down[:, own_lanes], preferred_element_type=F32)
            add_their += jnp.dot(hidden, down[:, far_lanes], preferred_element_type=F32)
        outgoing[n] = add_their.astype(BF)
        home(n).start()
        result_ref[rows, :] = add_own.astype(BF)
        return carry

    def finish(n, carry):
        home(n).wait()
        rows = rows_of(other, n)
        result_ref[rows, :] = (merged[rows, :] + returned[n].astype(F32)).astype(BF)
        return carry

    lax.fori_loop(0, PIECES, give, 0)
    lax.fori_loop(0, PIECES, keep, 0)
    hand_over().wait()
    lax.fori_loop(0, PIECES, mlp, 0)
    lax.fori_loop(0, PIECES, finish, 0)


def shards(
    features, positions, occupancy, neighbours, wavevectors, filters,
    falloffs, mixing, norm_gain, in_weight, out_weight,
):
    smem = pl.BlockSpec(memory_space=pltpu.SMEM)
    vmem = pl.BlockSpec(memory_space=pltpu.VMEM)
    hbm = pl.BlockSpec(memory_space=pl.ANY)
    half = (QUARTERS, 3, 4, 2, BLOCK, LANES)
    return pl.pallas_call(
        layer,
        in_specs=[smem] * 3 + [vmem] * 7 + [hbm],
        out_specs=vmem,
        out_shape=jax.ShapeDtypeStruct((ROWS, PART), BF),
        scratch_shapes=[
            pltpu.VMEM((LOCAL + 2 * HW, CAP, PART), BF),
            pltpu.VMEM((LOCAL + 2 * HW, 8, CAP), F32),
            pltpu.VMEM((TILES, 8, TILE), F32),
            pltpu.VMEM((ROWS, KP), BF),
            pltpu.VMEM((KP, TILE), BF),
            pltpu.VMEM((TILES, ROWS, TILE), BF),
            pltpu.VMEM((TILES, ROWS, TILE), BF),
            pltpu.VMEM((2, QUARTERS, 4, 4, 2, BLOCK, PART), BF),
            pltpu.VMEM((QUARTERS, 4, 4, 2, BLOCK, PART), BF),
            pltpu.VMEM(half, BF),
            pltpu.VMEM(half, BF),
            pltpu.VMEM((QUARTERS, 4, 2, BLOCK, LANES), BF),
            pltpu.VMEM((QUARTERS, 4, 2, BLOCK, LANES), BF),
            pltpu.VMEM((QUARTERS, 7, BLOCK, LANES), BF),
            pltpu.VMEM((QUARTERS, 7, BLOCK, LANES), BF),
            pltpu.VMEM((2, QUARTERS, 4, 4, 2, BLOCK, PART), BF),
            pltpu.VMEM((2, BLOCK, PART), F32),
            pltpu.VMEM((2, BLOCK, PART), F32),
            pltpu.VMEM((4, 8, LANES), F32),
            pltpu.VMEM((COUNTS, 8, LANES), F32),
            pltpu.VMEM((ROWS, PART), F32),
            pltpu.VMEM((2, *in_weight.shape), BF),
        ]
        + [pltpu.VMEM((PIECES, PIECE, PART), BF)] * 3
        + [pltpu.SemaphoreType.DMA((QUARTERS * MESSAGES,))] * 2
        + [pltpu.SemaphoreType.DMA((COUNTS,))] * 2
        + [pltpu.SemaphoreType.DMA((7,))] * 2
        + [pltpu.SemaphoreType.DMA((2 * PIECES,))] * 2
        + [pltpu.SemaphoreType.DMA((TILES + 1,))] * 2
        + [pltpu.SemaphoreType.DMA((2,))],
        compiler_params=params(collective_id=0, has_side_effects=True),
    )(
        occupancy, neighbours.reshape(LOCAL * NB), falloffs,
        features, positions, wavevectors, mixing, norm_gain[None, :],
        in_weight, out_weight, filters,
    )


def solution(mesh):
    placed = (
        P("cells", "waves"),
        P(None, "cells"),
        P("cells"),
        P("cells", None),
        P(None, "waves"),
        P("waves", None),
        P(),
        P(),
        P(),
        P(None, "waves"),
        P("waves", None),
    )
    return jax.shard_map(
        shards, mesh=mesh, in_specs=placed, out_specs=P("cells", "waves"), check_vma=False
    )
```
